32 devices in a mesh: row: 2 (over y), col: 16 (over z, x, core).
Axes of the slice: x: 2, y: 2, z: 4, core: 2. Of those that a mesh axis runs over, the one named last changes fastest.
Arguments:
- blocks: float32 [512, 128, 128], P(('row', 'col')), may hold values from -0.3125 to 0.3125
- block_row: int32 [512], P(('row', 'col')), may hold values from 0 to 63, as said below
- block_col: int32 [512], P(('row', 'col')), may hold values from 0 to 63, as said below
- counts: int32 [32], P(('row', 'col')), may hold values from 1 to 16, as said below
- diagonal: float32 [8192], P(('row', 'col')), may hold values from 0.25 to 4
- vector: float32 [8192, 256], P(('row', 'col')), may hold values from -8 to 8
Outputs:
- next_basis: float32 [8192, 256], P(('row', 'col'))
- second_image: float32 [8192, 256], P(('row', 'col'))
- arnoldi_column: float32 [2, 256], replicated
The draws below stay inside these ranges and needn't reach their ends.
Inputs may be any that keep to these rules, and one draw needn't show every extreme that they name: The slots of device d = r * 16 + c are rows d * 16 to (d + 1) * 16 - 1. Its slot d * 16 + k * 16 + o (k below 1) has block_row // 2 equal to r * 16 + o, and (block_col // 2) % 16 equals c. No pair (block_row, block_col) occurs twice among all slots. `block_col`: paired with block_row as stated there. Only the first counts[d] slots of device d hold blocks; later slots are ignored. Some device has exactly 16.
All inputs are finite; a program needn't handle non-finite values.
Results may differ from the reference program's by a relative error of at most 0.0001.
Values sent between devices are 32-bit elements; how exact they have to be, the bound alone decides.
A program may use at most 64 MiB of HBM per device.

```python
import math
import jax
import jax.numpy as jnp
from jax import lax

BLK = 128
VB = 2
CAP = 1
RHS = 256
MAXB = 16
NV = 8192
N_ROW = 2
N_COL = 16


def positions_of(key):
    device_count = N_ROW * N_COL
    choices_each = VB * N_ROW * VB
    keys = jax.random.split(jax.random.fold_in(key, 11), device_count * N_COL)

    def one_list(single):
        return jax.random.permutation(single, choices_each).astype(jnp.int32)[:CAP]
    spots = jax.vmap(one_list)(keys).astype(jnp.int32).reshape(device_count, N_COL, CAP)
    spots = jnp.transpose(spots, (0, 2, 1)).reshape(device_count, CAP * N_COL)
    device_ids = jnp.arange(device_count, dtype=jnp.int32)[:, None]
    grid_row = device_ids // N_COL
    grid_col = device_ids % N_COL
    target_col = (jnp.arange(CAP * N_COL, dtype=jnp.int32) % N_COL)[None, :]
    local_row = spots // (N_ROW * VB)
    local_col = spots % (N_ROW * VB)
    global_row = (grid_row * N_COL + target_col) * VB + local_row
    global_col = (local_col // VB * N_COL + grid_col) * VB + local_col % VB
    return (global_row.reshape(-1).astype(jnp.int32), global_col.reshape(-1).astype(jnp.int32))


def draw_block_row(key, part):
    return positions_of(key)[0]


def draw_block_col(key, part):
    return positions_of(key)[1]


def draw_counts(key, part):
    device_count = N_ROW * N_COL
    first_key, second_key, third_key = jax.random.split(jax.random.fold_in(key, 5), 3)
    exponent = jax.random.randint(first_key, (device_count,), 0, 4)
    base_count = MAXB // jnp.left_shift(jnp.ones((device_count,), jnp.int32), exponent)
    reduction = jax.random.randint(second_key, (device_count,), 0, base_count // 2 + 1)
    chosen = jnp.maximum(base_count - reduction, 1)
    busiest = jax.random.randint(third_key, (), 0, device_count)
    return jnp.where(jnp.arange(device_count) == busiest, MAXB, chosen).astype(jnp.int32)


def draw_vector(key, part):
    first_key = jax.random.fold_in(jax.random.fold_in(key, 3), 0)
    ramp = 0.6 + 1.2 * jnp.arange(NV, dtype=jnp.float32)[:, None] / NV
    values = jnp.clip(jax.random.normal(first_key, (NV, RHS), jnp.float32), -4.0, 4.0)
    return (values * ramp).astype(jnp.float32)


def steps_of(own_key, dims, pieces, low, high):
    loudness, own = 1.0, jax.random.fold_in(own_key, 6)
    for axis_at, blocks in pieces:
        draws = jnp.exp(jax.random.uniform(jax.random.fold_in(own, axis_at), (blocks,), jnp.float32, low / len(pieces), high / len(pieces)))
        loudness = loudness * jnp.repeat(draws, dims[axis_at] // blocks).reshape([-1 if axis == axis_at else 1 for axis in range(len(dims))])
    return loudness


def noise(rng, extent, width, bound, pieces=(), kind=jnp.bfloat16):
    array = width * jax.random.normal(rng, extent, jnp.float32)
    if pieces:
        array = array * steps_of(rng, extent, pieces, -0.22, 0.18)
    return jnp.clip(array, -bound, bound).astype(kind)


def setup_inputs(seed: int = 0) -> dict:
    streams_of = jax.random.split(jax.random.key(seed), 7)
    blocks = noise(streams_of[0], (N_ROW * N_COL * MAXB, BLK, BLK), (BLK * MAXB // (3 * VB)) ** -0.5, 0.3125, ((0, 32),), jnp.float32)
    block_row = draw_block_row(jax.random.fold_in(streams_of[6], 71), 0)
    block_col = draw_block_col(jax.random.fold_in(streams_of[6], 71), 0)
    counts = draw_counts(jax.random.fold_in(streams_of[6], 71), 0)
    diagonal = jnp.clip(jnp.exp(math.log(4.0) - 2.7725887 * jax.random.uniform(streams_of[4], (NV,), jnp.float32) ** steps_of(streams_of[4], (NV,), ((0, 32),), -0.2, 0.2)), 0.25, 4.0)
    vector = draw_vector(jax.random.fold_in(streams_of[6], 71), 0)
    return dict(blocks=blocks, block_row=block_row, block_col=block_col, counts=counts, diagonal=diagonal, vector=vector)


def apply_transpose(source, diagonal, blocks, block_row, block_col, counts):
    device_count = counts.shape[0]
    tile_size = blocks.shape[1]
    slot_count = blocks.shape[0] // device_count
    rhs_count = source.shape[1]
    block_total = source.shape[0] // tile_size
    stacked = source.reshape(block_total, tile_size, rhs_count)
    live_slot = (jnp.arange(slot_count, dtype=jnp.int32)[None, :] < counts[:, None]).astype(jnp.float32)

    def advance(totals, inputs):
        tile_set, row_ids, col_ids, weights = inputs
        picked = stacked[row_ids]
        products = jnp.einsum('mab,mak->mbk', tile_set, picked, precision=lax.Precision.HIGHEST)
        products = products * weights[:, None, None]
        return (totals.at[col_ids].add(products), None)
    start_sum = jnp.zeros((block_total, tile_size, rhs_count), jnp.float32)
    totals, _ = lax.scan(advance, start_sum, (blocks.reshape(device_count, slot_count, tile_size, tile_size), block_row.reshape(device_count, slot_count), block_col.reshape(device_count, slot_count), live_slot))
    return diagonal[:, None] * source + totals.reshape(source.shape)

def reference(blocks, block_row, block_col, counts, diagonal, vector):
    magnitude = jnp.sqrt(lax.optimization_barrier(jnp.mean(vector * vector, axis=0)) + 1e-06)
    unit_basis = vector / magnitude
    first_image = apply_transpose(unit_basis, diagonal, blocks, block_row, block_col, counts)
    projection = lax.optimization_barrier(jnp.mean(first_image * unit_basis, axis=0))
    remainder = first_image - projection * unit_basis
    norm_new = jnp.sqrt(lax.optimization_barrier(jnp.mean(remainder * remainder, axis=0)) + 1e-06)
    next_basis = remainder / norm_new
    second_image = apply_transpose(next_basis, diagonal, blocks, block_row, block_col, counts)
    return (next_basis, second_image, jnp.stack([projection, norm_new]))
```

```python
import functools

import jax
import jax.numpy as jnp
from jax import lax
from jax.experimental import pallas as pl
from jax.experimental.pallas import tpu as pltpu
from jax.sharding import PartitionSpec as P

MESH = pl.DeviceIdType.MESH
LANES = 128
ROWS = 8
CORES = 2


def chip_grid(chips):
    x = max(d for d in range(1, chips + 1) if chips % d == 0 and d * d <= chips)
    return chips // x, x


def nearest(turn, here, size):
    both = jnp.minimum(here, size - 1 - here)
    reach = (turn + 1) // 2
    near = jnp.where(turn % 2 == 1, here + reach, here - reach)
    far = jnp.where(here < size - 1 - here, turn, size - 1 - turn)
    return jnp.where(turn <= 2 * both, near, far)


def split(value):
    high = value.astype(jnp.bfloat16)
    low = (value - high.astype(jnp.float32)).astype(jnp.bfloat16)
    return high, low


def kernel(
    n_rows, n_cols, total_rows,
    brow, bcol, counts, blocks_hbm, diag_ref, vec_hbm,
    next_ref, second_ref, column_ref,
    blocks, held, weight, totals, partner, final, diag, meta, own_other, cross, side, stat_col, stat_row,
    local_sem, swap_send, swap_recv, unit_send, unit_recv, y_send, y_recv, fin_send, fin_recv,
    cross_sem, side_sem, col_send, col_recv, row_send, row_recv,
):
    slots, tile = blocks.shape[1], blocks.shape[2]
    cap = slots // n_cols
    per = held.shape[2]
    n_local = n_rows * per
    chips = n_cols // CORES
    size_z, size_x = chip_grid(chips)
    row, col = lax.axis_index("row"), lax.axis_index("col")
    core, chip = col % CORES, col // CORES
    mate = chip * CORES + 1 - core
    at_x, at_z = chip % size_x, chip // size_x
    mine_at = pl.ds(pl.multiple_of(core * LANES, LANES), LANES)
    other_at = pl.ds(pl.multiple_of((1 - core) * LANES, LANES), LANES)

    own, kept = [], []
    for b in range(per):
        at = pl.ds(b * tile, tile)
        own.append(pltpu.make_async_copy(vec_hbm.at[at, mine_at], held.at[0, col, b], local_sem.at[b]))
        kept.append(pltpu.make_async_copy(vec_hbm.at[at, other_at], own_other.at[b], local_sem.at[per + b]))
    kept.append(pltpu.make_async_copy(blocks_hbm, blocks.at[core], local_sem.at[2 * per]))
    for copy in own + kept:
        copy.start()

    barrier = pltpu.get_barrier_semaphore()

    @pl.loop(1, n_cols)
    def _(step):
        pl.semaphore_signal(barrier, inc=1, device_id=(row, (col + step) % n_cols), device_id_type=MESH)

    @pl.loop(1, n_rows)
    def _(step):
        there = (row + step) % n_rows
        pl.semaphore_signal(barrier, inc=1, device_id=(there, col), device_id_type=MESH)
        pl.semaphore_signal(barrier, inc=1, device_id=(there, mate), device_id_type=MESH)

    @pl.loop(0, slots)
    def _(slot):
        piece = bcol[slot] // per
        target = piece // n_cols * per + bcol[slot] % per
        target = jnp.where(slot < counts[0], target, -1)
        meta[core, slot, 0] = jnp.full((ROWS, LANES), target.astype(jnp.float32))
        meta[core, slot, 1] = jnp.full((ROWS, LANES), (brow[slot] % per).astype(jnp.float32))

    filler = jnp.zeros((ROWS - per, LANES), jnp.float32)
    meta[core, slots, 0] = jnp.concatenate([diag_ref[...], filler], axis=0)
    meta[core, slots, 1] = jnp.zeros((ROWS, LANES), jnp.float32)
    totals[...] = jnp.zeros_like(totals)
    pl.semaphore_wait(barrier, n_cols - 1 + 2 * (n_rows - 1))

    swaps = []

    def swap(source, target):
        i = len(swaps)
        swaps.append(pltpu.make_async_remote_copy(
            source, target, swap_send.at[i], swap_recv.at[i], device_id=(row, mate), device_id_type=MESH))

    for b in range(per):
        swap(vec_hbm.at[pl.ds(b * tile, tile), other_at], held.at[0, col, b])
    swap(meta.at[core], meta.at[core])
    swap(blocks_hbm, blocks.at[core])

    def edge(sz):
        return (sz == 0) | (sz == size_z - 1)

    def x_first(sz, part):
        if size_x == 1 or size_z == 1:
            return sz < 0
        return edge(sz) & (part == CORES - 1)

    def branches(g, sz, sx, part, act):
        o = (sz * size_x + sx) * CORES + part
        early = x_first(sz, part)
        along_z = early | (at_x == sx)
        along_x = jnp.logical_not(early) | (at_z == sz)
        targets = (
            (along_z & (at_z >= sz) & (at_z + 1 < size_z), at_x, at_z + 1),
            (along_z & (at_z <= sz) & (at_z >= 1), at_x, at_z - 1),
            (along_x & (at_x >= sx) & (at_x + 1 < size_x), at_x + 1, at_z),
            (along_x & (at_x <= sx) & (at_x >= 1), at_x - 1, at_z),
        )
        piece = held.at[g, o]
        for i, (wanted, tx, tz) in enumerate(targets):
            def go(i=i, tx=tx, tz=tz):
                act(pltpu.make_async_remote_copy(
                    piece, piece, unit_send.at[g, o, i], unit_recv.at[g, o],
                    device_id=(row, (tz * size_x + tx) * CORES + core), device_id_type=MESH))
            pl.when(wanted)(go)

    def start(copy):
        copy.start()

    def drain(copy):
        copy.wait_send()

    def relay(g, sz, sx, part):
        o = (sz * size_x + sx) * CORES + part
        piece = held.at[g, o]
        pltpu.make_async_remote_copy(
            piece, piece, unit_send.at[g, o, 0], unit_recv.at[g, o],
            device_id=(row, col), device_id_type=MESH).wait_recv()
        branches(g, sz, sx, part, start)

    def build(o):
        for q in range(cap):
            slot = q * n_cols + o
            for c in range(CORES):
                block = blocks[c, slot].T.reshape(tile // ROWS, ROWS, LANES)
                for b in range(per):
                    keep = (meta[c, slot, 1] == float(b))[None]
                    high, low = split(jnp.where(keep, block, 0.0).reshape(tile, tile))
                    weight[o, q, pl.ds(c * tile, tile), pl.ds(b * tile, tile)] = high
                    weight[o, q, pl.ds(c * tile, tile), pl.ds((per + b) * tile, tile)] = low

    def multiply(g, o):
        high, low = split(held[g, o].reshape(per * tile, LANES))
        both = jnp.concatenate([high, low], axis=1)
        both = jnp.concatenate([both, both], axis=0)
        for q in range(cap):
            slot = q * n_cols + o
            product = jnp.dot(weight[o, q], both, preferred_element_type=jnp.float32)
            product = product[:, :LANES] + product[:, LANES:]
            product = product.reshape(CORES, tile // ROWS, ROWS, LANES)
            for c in range(CORES):
                target = meta[c, slot, 0]
                for j in range(n_local):
                    add = jnp.where((target == float(j))[None], product[c], 0.0)
                    totals[g, c, j // per, j % per] += add.reshape(tile, LANES)

    def place(turn):
        return nearest(turn % size_z, at_z, size_z), nearest(turn // size_z, at_x, size_x)

    def consume(g, turn):
        sz, sx = place(turn)
        for part in range(CORES):
            o = (sz * size_x + sx) * CORES + part
            if g == 0:
                build(o)
            multiply(g, o)

    def ahead(turn, sz, part):
        return x_first(sz, part) & ((turn % size_z == 0) | jnp.logical_not(edge(at_z)))

    def relay_ahead(g, turn):
        sz = nearest(turn % size_z, at_z, size_z)
        for ux in range(1, size_x):
            part = CORES - 1
            pl.when(ahead(turn, sz, part))(
                lambda: relay(g, sz, nearest(ux, at_x, size_x), part))

    def relay_turn(g, turn):
        sz, sx = place(turn)
        for part in range(CORES):
            held_back = (turn < size_z) | jnp.logical_not(ahead(turn, sz, part))
            pl.when(held_back)(lambda: relay(g, sz, sx, part))

    def turns(g, low, high):
        @pl.loop(low, high)
        def _(turn):
            relay_turn(g, turn)
            pl.when(turn < size_z)(lambda: relay_ahead(g, turn))
            consume(g, turn - 1)

    def y_copy(c, step):
        target = (row + step) % n_rows
        return pltpu.make_async_remote_copy(
            totals.at[0, c, target], partner.at[c, row], y_send.at[c, step - 1], y_recv.at[c, step - 1],
            device_id=(target, col), device_id_type=MESH)

    def y_sum(c):
        total = totals[0, c, row]
        for step in range(1, n_rows):
            origin = (row + n_rows - step) % n_rows
            pltpu.make_async_remote_copy(
                totals.at[0, c, row], partner.at[c, origin], y_send.at[c, step - 1], y_recv.at[c, step - 1],
                device_id=(row, col), device_id_type=MESH).wait_recv()
            total = total + partner[c, origin]
        return total

    def fin_copies():
        copies = []
        for away in range(CORES):
            c = (core + away) % CORES
            for step in range(n_rows):
                if away or step:
                    target = (row + step) % n_rows
                    i = away * n_rows + step
                    copies.append(pltpu.make_async_remote_copy(
                        totals.at[1, c, target], final.at[away, row], fin_send.at[i], fin_recv.at[i],
                        device_id=(target, chip * CORES + c), device_id_type=MESH))
        return copies

    def fin_sum(away):
        total = None if away else totals[1, core, row]
        for step in range(n_rows):
            if away or step:
                origin = (row + n_rows - step) % n_rows
                i = away * n_rows + step
                pltpu.make_async_remote_copy(
                    totals.at[1, core, row], final.at[away, origin], fin_send.at[i], fin_recv.at[i],
                    device_id=(row, col), device_id_type=MESH).wait_recv()
                piece = final[away, origin]
                total = piece if total is None else total + piece
        return total

    def stats_begin(i, rows):
        filler = jnp.zeros((ROWS - len(rows), LANES), jnp.float32)
        stat_col[i, chip] = jnp.concatenate(list(rows) + [filler], axis=0)

        @pl.loop(1, chips)
        def _(step):
            pltpu.make_async_remote_copy(
                stat_col.at[i, chip], stat_col.at[i, chip], col_send.at[i], col_recv.at[i],
                device_id=(row, (chip + step) % chips * CORES + core), device_id_type=MESH).start()

    def stats_turn(i):
        many = stat_col.at[i, pl.ds(0, chips - 1)]
        pltpu.make_async_copy(many, many, col_recv.at[i]).wait()
        stat_row[i, row] = jnp.sum(stat_col[i], axis=0)

        @pl.loop(1, n_rows)
        def _(step):
            pltpu.make_async_remote_copy(
                stat_row.at[i, row], stat_row.at[i, row], row_send.at[i], row_recv.at[i],
                device_id=((row + step) % n_rows, col), device_id_type=MESH).start()

    def stats_end(i):
        many = stat_row.at[i, pl.ds(0, n_rows - 1)]
        pltpu.make_async_copy(many, many, row_recv.at[i]).wait()
        return jnp.sum(stat_row[i], axis=0)

    def stats_drain(i):
        many = stat_col.at[i, pl.ds(0, chips - 1)]
        pltpu.make_async_copy(many, many, col_send.at[i]).wait()
        many = stat_row.at[i, pl.ds(0, n_rows - 1)]
        pltpu.make_async_copy(many, many, row_send.at[i]).wait()

    def over_rows(value):
        return jnp.sum(value.reshape(per * tile, LANES), axis=0, keepdims=True)

    def drain_units(g):
        @pl.loop(0, chips)
        def _(p):
            for part in range(CORES):
                branches(g, p // size_x, p % size_x, part, drain)

    for copy in swaps[:per]:
        copy.start()
    for copy in own:
        copy.wait()
    branches(0, at_z, at_x, core, start)
    for copy in swaps[per:]:
        copy.start()
    for copy in swaps[:per]:
        copy.wait_recv()
    branches(0, at_z, at_x, 1 - core, start)
    squares = 0.0
    for c in range(CORES):
        rows = held[0, chip * CORES + c]
        squares += over_rows(rows * rows)
    stats_begin(0, [squares])
    swaps[per].wait_recv()
    for c in range(CORES):
        for b in range(per):
            diag[c, b] = jnp.broadcast_to(meta[c, slots, 0, pl.ds(b, 1)], (tile, LANES)).T
    relay_ahead(0, 0)
    for copy in kept:
        copy.wait()
    swaps[per + 1].wait_recv()
    turns(0, 1, size_z)
    stats_turn(0)
    turns(0, size_z, chips)
    total_squares = stats_end(0)[:1]
    magnitude = jnp.sqrt(total_squares / total_rows + 1e-06)
    consume(0, chips - 1)
    for c in range(CORES):
        for step in range(1, n_rows):
            y_copy(c, step).start()

    image_squares, crossed = 0.0, 0.0
    for c in range(CORES):
        rows = held[0, chip * CORES + c]
        image = (diag[c] * rows + y_sum(c)) / magnitude
        held[1, chip * CORES + c] = image
        branches(1, at_z, at_x, c, start)
        image_squares += over_rows(image * image)
        crossed += over_rows(image * (rows / magnitude))
    to_mate = pltpu.make_async_remote_copy(
        held.at[1, mate], cross, cross_sem.at[0], cross_sem.at[1], device_id=(row, mate), device_id_type=MESH)
    to_mate.start()
    stats_begin(1, [image_squares, crossed])
    relay_ahead(1, 0)
    turns(1, 1, size_z)
    stats_turn(1)
    turns(1, size_z, chips - 1)
    stats = stats_end(1)
    image_squares, crossed = stats[:1], stats[1:2]
    basis_squares = total_squares / (magnitude * magnitude)
    projection = crossed / total_rows
    power = (image_squares - 2.0 * projection * crossed + projection * projection * basis_squares) / total_rows
    norm_new = jnp.sqrt(jnp.maximum(power, 0.0) + 1e-06)
    side[core] = jnp.concatenate(
        [projection, norm_new, magnitude, jnp.zeros((ROWS - 3, LANES), jnp.float32)], axis=0)
    to_side = pltpu.make_async_remote_copy(
        side.at[core], side.at[core], side_sem.at[0], side_sem.at[1], device_id=(row, mate), device_id_type=MESH)
    to_side.start()
    turns(1, chips - 1, chips)
    to_mate.wait_recv()
    to_side.wait_recv()
    halves = []
    for away, at in ((0, mine_at), (1, other_at)):
        values = side[(core + away) % CORES]
        projection, norm_new, magnitude = values[:1], values[1:2], values[2:3]
        image = cross[...] if away else held[1, col]
        basis = (own_other[...] if away else held[0, col]) / magnitude
        next_ref[:, at] = ((image - projection * basis) / norm_new).reshape(per * tile, LANES)
        column_ref[:, at] = values[:2]
        halves.append((away, at, projection, norm_new, image))
    consume(1, chips - 1)
    sent = fin_copies()
    for copy in sent:
        copy.start()

    drain_units(0)
    drain_units(1)
    for g in range(2):
        stats_drain(g)
    for copy in swaps:
        copy.wait_send()
    to_mate.wait_send()
    to_side.wait_send()
    for c in range(CORES):
        for step in range(1, n_rows):
            y_copy(c, step).wait_send()
    for away, at, projection, norm_new, image in halves:
        result = (diag[core] * image + fin_sum(away) - projection * image) / norm_new
        second_ref[:, at] = result.reshape(per * tile, LANES)
    for copy in sent:
        copy.wait_send()


def per_device(blocks, block_row, block_col, counts, diagonal, vector):
    n_rows, n_cols = lax.axis_size("row"), lax.axis_size("col")
    slots, tile, _ = blocks.shape
    mine, rhs = vector.shape
    if rhs != CORES * LANES or tile != LANES:
        raise ValueError("shapes")
    per = mine // tile
    cap, chips = slots // n_cols, n_cols // CORES
    smem = pl.BlockSpec(memory_space=pltpu.SMEM)
    vmem = pl.BlockSpec(memory_space=pltpu.VMEM)
    anywhere = pl.BlockSpec(memory_space=pl.ANY)
    f32, dma = jnp.float32, pltpu.SemaphoreType.DMA
    rows = (per, tile, LANES)
    return pl.pallas_call(
        functools.partial(kernel, n_rows, n_cols, mine * n_rows * n_cols),
        out_shape=(
            jax.ShapeDtypeStruct((mine, rhs), f32),
            jax.ShapeDtypeStruct((mine, rhs), f32),
            jax.ShapeDtypeStruct((2, rhs), f32),
        ),
        in_specs=[smem, smem, smem, anywhere, vmem, anywhere],
        out_specs=(vmem, vmem, vmem),
        scratch_shapes=[
            pltpu.VMEM((CORES, slots, tile, tile), f32),
            pltpu.VMEM((2, n_cols) + rows, f32),
            pltpu.VMEM((n_cols, cap, CORES * tile, 2 * per * tile), jnp.bfloat16),
            pltpu.VMEM((2, CORES, n_rows) + rows, f32),
            pltpu.VMEM((CORES, n_rows) + rows, f32),
            pltpu.VMEM((CORES, n_rows) + rows, f32),
            pltpu.VMEM((CORES,) + rows, f32),
            pltpu.VMEM((CORES, slots + 1, 2, ROWS, LANES), f32),
            pltpu.VMEM(rows, f32),
            pltpu.VMEM(rows, f32),
            pltpu.VMEM((CORES, ROWS, LANES), f32),
            pltpu.VMEM((2, chips, ROWS, LANES), f32),
            pltpu.VMEM((2, n_rows, ROWS, LANES), f32),
            dma((2 * per + 1,)),
            dma((per + 2,)), dma((per + 2,)),
            dma((2, n_cols, 4)), dma((2, n_cols)),
            dma((CORES, n_rows)), dma((CORES, n_rows)),
            dma((CORES * n_rows,)), dma((CORES * n_rows,)),
            dma((2,)), dma((2,)),
            dma((2,)), dma((2,)), dma((2,)), dma((2,)),
        ],
        compiler_params=pltpu.CompilerParams(
            collective_id=0, has_side_effects=True, vmem_limit_bytes=60 * 1024 * 1024),
    )(block_row, block_col, counts, blocks, diagonal.reshape(per, tile), vector)


def solution(mesh):
    spec = P(("row", "col"))
    return jax.shard_map(
        per_device,
        mesh=mesh,
        in_specs=(P(("row", "col"), None, None), spec, spec, spec, spec, P(("row", "col"), None)),
        out_specs=(P(("row", "col"), None), P(("row", "col"), None), P()),
        check_vma=False,
    )
```

```python
import functools

import jax
import jax.numpy as jnp
from jax import lax
from jax.experimental import pallas as pl
from jax.experimental.pallas import tpu as pltpu
from jax.sharding import PartitionSpec as P

MESH = pl.DeviceIdType.MESH
LANES = 128
ROWS = 8
CORES = 2
HALF = LANES // 2
PARTS = LANES // HALF


def chip_grid(chips):
    x = max(d for d in range(1, chips + 1) if chips % d == 0 and d * d <= chips)
    return chips // x, x


def nearest(turn, here, size):
    both = jnp.minimum(here, size - 1 - here)
    reach = (turn + 1) // 2
    near = jnp.where(turn % 2 == 1, here + reach, here - reach)
    far = jnp.where(here < size - 1 - here, turn, size - 1 - turn)
    return jnp.where(turn <= 2 * both, near, far)


def split(value):
    high = value.astype(jnp.bfloat16)
    low = (value - high.astype(jnp.float32)).astype(jnp.bfloat16)
    return high, low


def roll(value):
    return pltpu.roll(value, HALF, 1)


def kernel(
    n_rows, n_cols, total_rows,
    brow, bcol, counts, blocks_hbm, diag_ref, vec_hbm,
    next_ref, second_ref, column_ref,
    blocks, held, weight, totals, packed, partner, final, diag, meta, raw, own_other, cross, result, side,
    stat_col, stat_row,
    local_sem, swap_send, swap_recv, unit_send, unit_recv, y_send, y_recv, fin_send, fin_recv,
    cross_send, cross_recv, side_sem, col_send, col_recv, row_send, row_recv,
):
    slots, tile = blocks.shape[1], blocks.shape[2]
    cap = slots // n_cols
    per = raw.shape[1]
    n_local = n_rows * per
    chips = n_cols // CORES
    size_z, size_x = chip_grid(chips)
    row, col = lax.axis_index("row"), lax.axis_index("col")
    core, chip = col % CORES, col // CORES
    mate = chip * CORES + 1 - core
    at_x, at_z = chip % size_x, chip // size_x
    mine_at = pl.ds(pl.multiple_of(core * LANES, LANES), LANES)
    other_at = pl.ds(pl.multiple_of((1 - core) * LANES, LANES), LANES)
    low_lane = lax.broadcasted_iota(jnp.int32, (ROWS, LANES), 1) < HALF
    low_row = low_lane[:1]

    own, kept = [], []
    for b in range(per):
        at = pl.ds(b * tile, tile)
        own.append(pltpu.make_async_copy(vec_hbm.at[at, mine_at], raw.at[core, b], local_sem.at[b]))
        kept.append(pltpu.make_async_copy(vec_hbm.at[at, other_at], own_other.at[b], local_sem.at[per + b]))
    kept.append(pltpu.make_async_copy(blocks_hbm, blocks.at[core], local_sem.at[2 * per]))
    for copy in own + kept:
        copy.start()

    barrier = pltpu.get_barrier_semaphore()

    @pl.loop(1, n_cols)
    def _(step):
        pl.semaphore_signal(barrier, inc=1, device_id=(row, (col + step) % n_cols), device_id_type=MESH)

    @pl.loop(1, n_rows)
    def _(step):
        there = (row + step) % n_rows
        pl.semaphore_signal(barrier, inc=1, device_id=(there, col), device_id_type=MESH)
        pl.semaphore_signal(barrier, inc=1, device_id=(there, mate), device_id_type=MESH)

    @pl.loop(0, slots)
    def _(slot):
        piece = bcol[slot] // per
        target = piece // n_cols * per + bcol[slot] % per
        target = jnp.where(slot < counts[0], target, -1)
        reads_low = jnp.where(low_lane, 0, 1) == brow[slot] % per
        meta[core, slot] = jnp.where(reads_low, target, -1).astype(jnp.float32)

    filler = jnp.zeros((ROWS - per, LANES), jnp.float32)
    meta[core, slots] = jnp.concatenate([diag_ref[...], filler], axis=0)
    totals[...] = jnp.zeros_like(totals)
    pl.semaphore_wait(barrier, n_cols - 1 + 2 * (n_rows - 1))

    swaps = []

    def swap(source, target):
        i = len(swaps)
        swaps.append(pltpu.make_async_remote_copy(
            source, target, swap_send.at[i], swap_recv.at[i], device_id=(row, mate), device_id_type=MESH))

    for b in range(per):
        swap(vec_hbm.at[pl.ds(b * tile, tile), other_at], raw.at[core, b])
    swap(meta.at[core], meta.at[core])
    swap(blocks_hbm, blocks.at[core])

    def lanes_of(low, high):
        keep = low_row if low.shape[0] == 1 else low_lane
        shape = low.shape
        low, high = low.reshape((-1,) + keep.shape), high.reshape((-1,) + keep.shape)
        return jnp.where(keep[None], low, high).reshape(shape)

    def pack(first, second):
        return lanes_of(first, roll(second)), lanes_of(roll(first), second)

    def at_unit(g, s, o):
        return (g * PARTS + s) * n_cols + o

    def edge(sz):
        return (sz == 0) | (sz == size_z - 1)

    turned = size_x > 1 and size_z > 1

    def x_first(sz, part):
        return edge(sz) & (part == CORES - 1) if turned else sz < 0

    def branches(g, s, sz, sx, part, spread=False):
        o = (sz * size_x + sx) * CORES + part
        along_z = at_x == sx
        along_x = jnp.logical_not(x_first(sz, part)) | (at_z == sz)
        targets = [
            (0, along_z & (at_z >= sz) & (at_z + 1 < size_z), at_x, at_z + 1),
            (1, along_z & (at_z <= sz) & (at_z >= 1), at_x, at_z - 1),
            (2, along_x & (at_x >= sx) & (at_x + 1 < size_x), at_x + 1, at_z),
            (3, along_x & (at_x <= sx) & (at_x >= 1), at_x - 1, at_z),
        ]
        if spread:
            targets = targets[2:]
            for step in range(1, size_z):
                targets += [(0, at_z == 0, at_x, step), (1, at_z == size_z - 1, at_x, size_z - 1 - step)]
        piece = held.at[at_unit(g, s, o)]
        for i, wanted, tx, tz in targets:
            def go(i=i, tx=tx, tz=tz):
                pltpu.make_async_remote_copy(
                    piece, piece, unit_send.at[i], unit_recv.at[at_unit(g, s, o)],
                    device_id=(row, (tz * size_x + tx) * CORES + core), device_id_type=MESH).start()
            pl.when(wanted)(go)

    def drain_units():
        ahead_parts = size_x - 1 if turned else 0

        def wait(i, n, wanted):
            def go():
                many = held.at[pl.ds(0, 2 * PARTS * n)]
                pltpu.make_async_copy(many, many, unit_send.at[i]).wait()
            pl.when(wanted)(go)

        for v in range(size_z - 1):
            n = (v + 1) * CORES + (ahead_parts * (size_z - 1) if v == 0 else 0)
            wait(0, n, at_z == v)
            wait(1, n, at_z == size_z - 1 - v)
        for v in range(size_x - 1):
            for at_edge in (0, 1):
                n = (v + 1) * (CORES * size_z - (2 - at_edge if turned else 0))
                here = edge(at_z) if at_edge else jnp.logical_not(edge(at_z))
                wait(2, n, here & (at_x == v))
                wait(3, n, here & (at_x == size_x - 1 - v))

    def relay(g, s, sz, sx, part, spread=False):
        unit = at_unit(g, s, (sz * size_x + sx) * CORES + part)
        piece = held.at[unit]
        pltpu.make_async_remote_copy(
            piece, piece, unit_send.at[0], unit_recv.at[unit],
            device_id=(row, col), device_id_type=MESH).wait_recv()
        branches(g, s, sz, sx, part, spread)

    def build(o):
        for q in range(cap):
            slot = q * n_cols + o
            for c in range(CORES):
                high, low = split(blocks[c, slot].T)
                weight[o, q, pl.ds(c * tile, tile), pl.ds(0, tile)] = high
                weight[o, q, pl.ds(c * tile, tile), pl.ds(tile, tile)] = low

    def multiply(g, s, o):
        both = jnp.concatenate(split(held[at_unit(g, s, o)]), axis=1)
        both = jnp.concatenate([both, both], axis=0)
        for q in range(cap):
            slot = q * n_cols + o
            product = jnp.dot(weight[o, q], both, preferred_element_type=jnp.float32)
            product = product[:, :LANES] + product[:, LANES:]
            product = product.reshape(CORES, tile // ROWS, ROWS, LANES)
            for c in range(CORES):
                target = meta[c, slot]
                for j in range(n_local):
                    add = jnp.where((target == float(j))[None], product[c], 0.0)
                    totals[g, s, c, j] += add.reshape(tile, LANES)

    def place(turn):
        return nearest(turn % size_z, at_z, size_z), nearest(turn // size_z, at_x, size_x)

    def consume(g, s, turn):
        sz, sx = place(turn)
        for part in range(CORES):
            o = (sz * size_x + sx) * CORES + part
            if g == 0 and s == 0:
                build(o)
            multiply(g, s, o)

    def ahead(turn, sz, part):
        return x_first(sz, part) & (turn % size_z == 0)

    def relay_ahead(g, s):
        for ux in range(1, size_x):
            part = CORES - 1
            pl.when(x_first(at_z, part))(
                lambda: relay(g, s, at_z, nearest(ux, at_x, size_x), part, spread=True))

    def relay_x(g, s, turn):
        sz, sx = place(turn)
        for part in range(CORES):
            pl.when(jnp.logical_not(ahead(turn, sz, part)))(lambda: relay(g, s, sz, sx, part))

    def relay_z(g, s, turn):
        sz, sx = place(turn)
        for part in range(CORES):
            relay(g, s, sz, sx, part)

    def x_turns(g, s):
        @pl.loop(size_z, chips - 1)
        def _(turn):
            relay_x(g, s, turn)
            consume(g, s, turn - 1)

    def fold(g, s):
        for c in range(CORES):
            for r in range(n_rows):
                sums = [totals[g, s, c, r * per + b] for b in range(per)]
                packed[g, s, c, r] = lanes_of(*[value + roll(value) for value in sums])

    def y_copy(s, c, step):
        target = (row + step) % n_rows
        return pltpu.make_async_remote_copy(
            packed.at[0, s, c, target], partner.at[s, c, row], y_send.at[s, c, step - 1], y_recv.at[s, c, step - 1],
            device_id=(target, col), device_id_type=MESH)

    def y_sum(s, c):
        total = packed[0, s, c, row]
        for step in range(1, n_rows):
            origin = (row + n_rows - step) % n_rows
            pltpu.make_async_remote_copy(
                packed.at[0, s, c, row], partner.at[s, c, origin], y_send.at[s, c, step - 1], y_recv.at[s, c, step - 1],
                device_id=(row, col), device_id_type=MESH).wait_recv()
            total = total + partner[s, c, origin]
        return total

    def fin_copies(s):
        copies = []
        for away in range(CORES):
            c = (core + away) % CORES
            for step in range(n_rows):
                if away or step:
                    target = (row + step) % n_rows
                    i = away * n_rows + step
                    copies.append(pltpu.make_async_remote_copy(
                        packed.at[1, s, c, target], final.at[s, away, row], fin_send.at[s, i], fin_recv.at[s, i],
                        device_id=(target, chip * CORES + c), device_id_type=MESH))
        return copies

    def fin_sum(s, away):
        total = None if away else packed[1, s, core, row]
        for step in range(n_rows):
            if away or step:
                origin = (row + n_rows - step) % n_rows
                i = away * n_rows + step
                pltpu.make_async_remote_copy(
                    packed.at[1, s, core, row], final.at[s, away, origin], fin_send.at[s, i], fin_recv.at[s, i],
                    device_id=(row, col), device_id_type=MESH).wait_recv()
                piece = final[s, away, origin]
                total = piece if total is None else total + piece
        return total

    def close(g, s):
        consume(g, s, chips - 1)
        fold(g, s)
        copies = fin_copies(s) if g else [y_copy(s, c, step) for c in range(CORES) for step in range(1, n_rows)]
        for copy in copies:
            copy.start()
        return copies

    def stats_begin(i, rows):
        filler = jnp.zeros((ROWS - len(rows), LANES), jnp.float32)
        stat_col[i, chip] = jnp.concatenate(list(rows) + [filler], axis=0)

        @pl.loop(1, chips)
        def _(step):
            pltpu.make_async_remote_copy(
                stat_col.at[i, chip], stat_col.at[i, chip], col_send.at[i], col_recv.at[i],
                device_id=(row, (chip + step) % chips * CORES + core), device_id_type=MESH).start()

    def stats_turn(i):
        many = stat_col.at[i, pl.ds(0, chips - 1)]
        pltpu.make_async_copy(many, many, col_recv.at[i]).wait()
        stat_row[i, row] = jnp.sum(stat_col[i], axis=0)

        @pl.loop(1, n_rows)
        def _(step):
            pltpu.make_async_remote_copy(
                stat_row.at[i, row], stat_row.at[i, row], row_send.at[i], row_recv.at[i],
                device_id=((row + step) % n_rows, col), device_id_type=MESH).start()

    def stats_end(i):
        many = stat_row.at[i, pl.ds(0, n_rows - 1)]
        pltpu.make_async_copy(many, many, row_recv.at[i]).wait()
        value = jnp.sum(stat_row[i], axis=0)
        return value + roll(value)

    def stats_drain(i):
        many = stat_col.at[i, pl.ds(0, chips - 1)]
        pltpu.make_async_copy(many, many, col_send.at[i]).wait()
        many = stat_row.at[i, pl.ds(0, n_rows - 1)]
        pltpu.make_async_copy(many, many, row_send.at[i]).wait()

    def over_rows(value):
        return jnp.sum(value, axis=0, keepdims=True)

    def pack_own(part):
        units = pack(*[raw[part, b] for b in range(per)])
        for s in range(PARTS):
            held[at_unit(0, s, chip * CORES + part)] = units[s]
        branches(0, 0, at_z, at_x, part)

    for copy in swaps[:per]:
        copy.start()
    for copy in own:
        copy.wait()
    pack_own(core)
    for copy in swaps[per:]:
        copy.start()
    for copy in swaps[:per]:
        copy.wait_recv()
    pack_own(1 - core)
    squares = []
    for s in range(PARTS):
        units = [held[at_unit(0, s, chip * CORES + c)] for c in range(CORES)]
        squares.append(sum(over_rows(unit * unit) for unit in units))
    stats_begin(0, squares)
    swaps[per].wait_recv()
    for c in range(CORES):
        columns = [jnp.broadcast_to(meta[c, slots, pl.ds(b, 1)], (tile, LANES)).T for b in range(per)]
        diag[c] = lanes_of(*columns)

    def open_first():
        for part in range(CORES):
            branches(0, 1, at_z, at_x, part)
        for copy in kept:
            copy.wait()
        swaps[per + 1].wait_recv()

    def gather(g, open_second, hooks):
        relay_z(g, 0, 1)
        relay_ahead(g, 0)
        open_second()
        @pl.loop(2, size_z)
        def _(turn):
            relay_z(g, 0, turn)
            consume(g, 0, turn - 2)
        relay_ahead(g, 1)
        consume(g, 0, size_z - 2)
        @pl.loop(1, size_z - 1)
        def _(turn):
            relay_z(g, 1, turn)
            consume(g, 1, turn - 1)
        hooks[0]()
        x_turns(g, 0)
        relay_x(g, 0, chips - 1)
        consume(g, 0, chips - 2)
        sent = close(g, 0)
        relay_z(g, 1, size_z - 1)
        consume(g, 1, size_z - 2)
        hooks[1]()
        x_turns(g, 1)
        hooks[2]()
        relay_x(g, 1, chips - 1)
        consume(g, 1, chips - 2)
        sent = sent + close(g, 1)
        return sent

    known = {}

    def nothing():
        pass

    def end_first_stats():
        stats = stats_end(0)
        known["squares"] = [stats[s:s + 1] for s in range(PARTS)]
        known["magnitude"] = [jnp.sqrt(stats[s:s + 1] / total_rows + 1e-06) for s in range(PARTS)]
        known["rows"] = []

    def make_image(s):
        image_squares, crossed = 0.0, 0.0
        magnitude = known["magnitude"][s]
        for c in range(CORES):
            unit = held[at_unit(0, s, chip * CORES + c)]
            image = (diag[c] * unit + y_sum(s, c)) / magnitude
            held[at_unit(1, s, chip * CORES + c)] = image
            branches(1, s, at_z, at_x, c)
            image_squares += over_rows(image * image)
            crossed += over_rows(image * (unit / magnitude))
        known["rows"] += [image_squares, crossed]
        to_mate(s).start()

    def to_mate(s):
        return pltpu.make_async_remote_copy(
            held.at[at_unit(1, s, mate)], cross.at[s], cross_send.at[s], cross_recv.at[s],
            device_id=(row, mate), device_id_type=MESH)

    y_sent = gather(0, open_first, (lambda: stats_turn(0), end_first_stats, lambda: make_image(0)))

    to_side = pltpu.make_async_remote_copy(
        side.at[core], side.at[core], side_sem.at[0], side_sem.at[1], device_id=(row, mate), device_id_type=MESH)

    def open_image():
        make_image(1)
        stats_begin(1, known["rows"])

    def end_second_stats():
        stats = stats_end(1)
        rows = []
        for s in range(PARTS):
            image_squares, crossed = stats[2 * s:2 * s + 1], stats[2 * s + 1:2 * s + 2]
            magnitude = known["magnitude"][s]
            basis_squares = known["squares"][s] / (magnitude * magnitude)
            projection = crossed / total_rows
            power = (image_squares - 2.0 * projection * crossed + projection * projection * basis_squares) / total_rows
            rows.append((projection, jnp.sqrt(jnp.maximum(power, 0.0) + 1e-06), magnitude))
        rows = [lanes_of(first, second) for first, second in zip(*rows)]
        side[core] = jnp.concatenate(rows + [jnp.zeros((ROWS - len(rows), LANES), jnp.float32)], axis=0)
        to_side.start()

    places = ((0, mine_at), (1, other_at))

    def image_of(s, away):
        return cross[s] if away else held[at_unit(1, s, col)]

    def make_next():
        to_side.wait_recv()
        for s in range(PARTS):
            to_mate(s).wait_recv()
        for away, at in places:
            values = side[(core + away) % CORES]
            projection, norm_new, magnitude = values[:1], values[1:2], values[2:3]
            images = pack(*[image_of(s, away) for s in range(PARTS)])
            for b in range(per):
                vector = own_other[b] if away else raw[core, b]
                basis = vector / magnitude
                next_ref[pl.ds(b * tile, tile), at] = (images[b] - projection * basis) / norm_new
            column_ref[:, at] = values[:2]

    def finish(s):
        for away, _ in places:
            values = side[(core + away) % CORES]
            values = lanes_of(values, roll(values)) if s == 0 else lanes_of(roll(values), values)
            image = image_of(s, away)
            result[s, away] = (diag[core] * image + fin_sum(s, away) - values[:1] * image) / values[1:2]

    sent = gather(1, open_image, (lambda: stats_turn(1), end_second_stats, make_next))

    finish(0)
    drain_units()
    for g in range(2):
        stats_drain(g)
    for copy in swaps + y_sent + [to_mate(s) for s in range(PARTS)] + [to_side]:
        copy.wait_send()
    finish(1)
    for away, at in places:
        values = pack(*[result[s, away] for s in range(PARTS)])
        for b in range(per):
            second_ref[pl.ds(b * tile, tile), at] = values[b]
    for copy in sent:
        copy.wait_send()


def per_device(blocks, block_row, block_col, counts, diagonal, vector):
    n_rows, n_cols = lax.axis_size("row"), lax.axis_size("col")
    slots, tile, _ = blocks.shape
    mine, rhs = vector.shape
    per = mine // tile
    if rhs != CORES * LANES or tile != LANES or per != PARTS:
        raise ValueError("shapes")
    cap, chips = slots // n_cols, n_cols // CORES
    smem = pl.BlockSpec(memory_space=pltpu.SMEM)
    vmem = pl.BlockSpec(memory_space=pltpu.VMEM)
    anywhere = pl.BlockSpec(memory_space=pl.ANY)
    f32, dma = jnp.float32, pltpu.SemaphoreType.DMA
    unit = (tile, LANES)
    return pl.pallas_call(
        functools.partial(kernel, n_rows, n_cols, mine * n_rows * n_cols),
        out_shape=(
            jax.ShapeDtypeStruct((mine, rhs), f32),
            jax.ShapeDtypeStruct((mine, rhs), f32),
            jax.ShapeDtypeStruct((2, rhs), f32),
        ),
        in_specs=[smem, smem, smem, anywhere, vmem, anywhere],
        out_specs=(vmem, vmem, vmem),
        scratch_shapes=[
            pltpu.VMEM((CORES, slots, tile, tile), f32),
            pltpu.VMEM((2 * PARTS * n_cols,) + unit, f32),
            pltpu.VMEM((n_cols, cap, CORES * tile, 2 * tile), jnp.bfloat16),
            pltpu.VMEM((2, PARTS, CORES, n_rows * per) + unit, f32),
            pltpu.VMEM((2, PARTS, CORES, n_rows) + unit, f32),
            pltpu.VMEM((PARTS, CORES, n_rows) + unit, f32),
            pltpu.VMEM((PARTS, CORES, n_rows) + unit, f32),
            pltpu.VMEM((CORES,) + unit, f32),
            pltpu.VMEM((CORES, slots + 1, ROWS, LANES), f32),
            pltpu.VMEM((CORES, per) + unit, f32),
            pltpu.VMEM((per,) + unit, f32),
            pltpu.VMEM((PARTS,) + unit, f32),
            pltpu.VMEM((PARTS, CORES) + unit, f32),
            pltpu.VMEM((CORES, ROWS, LANES), f32),
            pltpu.VMEM((2, chips, ROWS, LANES), f32),
            pltpu.VMEM((2, n_rows, ROWS, LANES), f32),
            dma((2 * per + 1,)),
            dma((per + 2,)), dma((per + 2,)),
            dma((4,)), dma((2 * PARTS * n_cols,)),
            dma((PARTS, CORES, n_rows - 1)), dma((PARTS, CORES, n_rows - 1)),
            dma((PARTS, CORES * n_rows)), dma((PARTS, CORES * n_rows)),
            dma((PARTS,)), dma((PARTS,)), dma((2,)),
            dma((2,)), dma((2,)), dma((2,)), dma((2,)),
        ],
        compiler_params=pltpu.CompilerParams(
            collective_id=0, has_side_effects=True, vmem_limit_bytes=60 * 1024 * 1024),
    )(block_row, block_col, counts, blocks, diagonal.reshape(per, tile), vector)


def solution(mesh):
    spec = P(("row", "col"))
    return jax.shard_map(
        per_device,
        mesh=mesh,
        in_specs=(P(("row", "col"), None, None), spec, spec, spec, spec, P(("row", "col"), None)),
        out_specs=(P(("row", "col"), None), P(("row", "col"), None), P()),
        check_vma=False,
    )
```

```python
import functools

import jax
import jax.numpy as jnp
from jax import lax
from jax.experimental import pallas as pl
from jax.experimental.pallas import tpu as pltpu
from jax.sharding import PartitionSpec as P

MESH = pl.DeviceIdType.MESH
LANES = 128
ROWS = 8
CORES = 2
HALF = LANES // 2
PARTS = LANES // HALF


def chip_grid(chips):
    x = max(d for d in range(1, chips + 1) if chips % d == 0 and d * d <= chips)
    return chips // x, x


def nearest(turn, here, size):
    both = jnp.minimum(here, size - 1 - here)
    reach = (turn + 1) // 2
    near = jnp.where(turn % 2 == 1, here + reach, here - reach)
    far = jnp.where(here < size - 1 - here, turn, size - 1 - turn)
    return jnp.where(turn <= 2 * both, near, far)


def split(value):
    high = value.astype(jnp.bfloat16)
    low = (value - high.astype(jnp.float32)).astype(jnp.bfloat16)
    return high, low


def roll(value):
    return pltpu.roll(value, HALF, 1)


def kernel(
    n_rows, n_cols, total_rows,
    brow, bcol, counts, blocks_hbm, diag_ref, vec_hbm,
    next_ref, second_ref, column_ref,
    blocks, held, weight, totals, packed, partner, final, diag, meta, raw, own_other, cross, result, side,
    stat_col, stat_row,
    local_sem, swap_send, swap_recv, unit_send, unit_recv, y_send, y_recv, fin_send, fin_recv,
    cross_send, cross_recv, side_sem, col_send, col_recv, row_send, row_recv,
):
    slots, tile = blocks.shape[1], blocks.shape[2]
    cap = slots // n_cols
    per = raw.shape[1]
    n_local = n_rows * per
    chips = n_cols // CORES
    size_z, size_x = chip_grid(chips)
    row, col = lax.axis_index("row"), lax.axis_index("col")
    core, chip = col % CORES, col // CORES
    mate = chip * CORES + 1 - core
    at_x, at_z = chip % size_x, chip // size_x
    mine_at = pl.ds(pl.multiple_of(core * LANES, LANES), LANES)
    other_at = pl.ds(pl.multiple_of((1 - core) * LANES, LANES), LANES)
    low_lane = lax.broadcasted_iota(jnp.int32, (ROWS, LANES), 1) < HALF
    low_row = low_lane[:1]

    own, kept = [], []
    for b in range(per):
        at = pl.ds(b * tile, tile)
        own.append(pltpu.make_async_copy(vec_hbm.at[at, mine_at], raw.at[core, b], local_sem.at[b]))
        kept.append(pltpu.make_async_copy(vec_hbm.at[at, other_at], own_other.at[b], local_sem.at[per + b]))
    kept.append(pltpu.make_async_copy(blocks_hbm, blocks.at[core], local_sem.at[2 * per]))
    for copy in own + kept:
        copy.start()

    barrier = pltpu.get_barrier_semaphore()

    @pl.loop(1, n_cols)
    def _(step):
        pl.semaphore_signal(barrier, inc=1, device_id=(row, (col + step) % n_cols), device_id_type=MESH)

    @pl.loop(1, n_rows)
    def _(step):
        there = (row + step) % n_rows
        pl.semaphore_signal(barrier, inc=1, device_id=(there, col), device_id_type=MESH)
        pl.semaphore_signal(barrier, inc=1, device_id=(there, mate), device_id_type=MESH)

    @pl.loop(0, slots)
    def _(slot):
        piece = bcol[slot] // per
        target = piece // n_cols * per + bcol[slot] % per
        target = jnp.where(slot < counts[0], target, -1)
        reads_low = jnp.where(low_lane, 0, 1) == brow[slot] % per
        meta[core, slot] = jnp.where(reads_low, target, -1).astype(jnp.float32)

    filler = jnp.zeros((ROWS - per, LANES), jnp.float32)
    meta[core, slots] = jnp.concatenate([diag_ref[...], filler], axis=0)
    totals[...] = jnp.zeros_like(totals)
    pl.semaphore_wait(barrier, n_cols - 1 + 2 * (n_rows - 1))

    swaps = []

    def swap(source, target):
        i = len(swaps)
        swaps.append(pltpu.make_async_remote_copy(
            source, target, swap_send.at[i], swap_recv.at[i], device_id=(row, mate), device_id_type=MESH))

    for b in range(per):
        swap(vec_hbm.at[pl.ds(b * tile, tile), other_at], raw.at[core, b])
    swap(meta.at[core], meta.at[core])
    swap(blocks_hbm, blocks.at[core])

    def lanes_of(low, high):
        keep = low_row if low.shape[0] == 1 else low_lane
        shape = low.shape
        low, high = low.reshape((-1,) + keep.shape), high.reshape((-1,) + keep.shape)
        return jnp.where(keep[None], low, high).reshape(shape)

    def pack(first, second):
        return lanes_of(first, roll(second)), lanes_of(roll(first), second)

    def at_unit(g, s, o):
        return (g * PARTS + s) * n_cols + o

    turned = size_x > 1 and size_z % 2 == 0

    def beside(z):
        return z + 1 - 2 * (z % 2)

    def by_row(part):
        return (part == CORES - 1) if turned else (part < 0)

    def branches(g, s, sz, sx, part, spread=False):
        o = (sz * size_x + sx) * CORES + part
        along_z = at_x == sx
        along_x = jnp.logical_not(by_row(part) & (sz == beside(at_z)))
        targets = [
            (0, along_z & (at_z >= sz) & (at_z + 1 < size_z), at_x, at_z + 1),
            (1, along_z & (at_z <= sz) & (at_z >= 1), at_x, at_z - 1),
            (2, along_x & (at_x >= sx) & (at_x + 1 < size_x), at_x + 1, at_z),
            (3, along_x & (at_x <= sx) & (at_x >= 1), at_x - 1, at_z),
        ]
        if spread:
            targets = targets[2:]
            targets += [(0, at_z % 2 == 0, at_x, at_z + 1), (1, at_z % 2 == 1, at_x, at_z - 1)]
        piece = held.at[at_unit(g, s, o)]
        for i, wanted, tx, tz in targets:
            def go(i=i, tx=tx, tz=tz):
                pltpu.make_async_remote_copy(
                    piece, piece, unit_send.at[i], unit_recv.at[at_unit(g, s, o)],
                    device_id=(row, (tz * size_x + tx) * CORES + core), device_id_type=MESH).start()
            pl.when(wanted)(go)

    def drain_units():
        extra = size_x - 1 if turned else 0

        def wait(i, n, wanted):
            def go():
                many = held.at[pl.ds(0, 2 * PARTS * n)]
                pltpu.make_async_copy(many, many, unit_send.at[i]).wait()
            pl.when(wanted)(go)

        for v in range(size_z):
            if v + 1 < size_z:
                wait(0, (v + 1) * CORES + (extra if v % 2 == 0 else 0), at_z == v)
            if v:
                wait(1, (size_z - v) * CORES + (extra if v % 2 else 0), at_z == v)
        for v in range(size_x - 1):
            n = (v + 1) * (CORES * size_z - (1 if turned else 0))
            wait(2, n, at_x == v)
            wait(3, n, at_x == size_x - 1 - v)

    def relay(g, s, sz, sx, part, spread=False):
        unit = at_unit(g, s, (sz * size_x + sx) * CORES + part)
        piece = held.at[unit]
        pltpu.make_async_remote_copy(
            piece, piece, unit_send.at[0], unit_recv.at[unit],
            device_id=(row, col), device_id_type=MESH).wait_recv()
        branches(g, s, sz, sx, part, spread)

    def build(o):
        for q in range(cap):
            slot = q * n_cols + o
            for c in range(CORES):
                high, low = split(blocks[c, slot].T)
                weight[o, q, pl.ds(c * tile, tile), pl.ds(0, tile)] = high
                weight[o, q, pl.ds(c * tile, tile), pl.ds(tile, tile)] = low

    def multiply(g, s, o):
        both = jnp.concatenate(split(held[at_unit(g, s, o)]), axis=1)
        both = jnp.concatenate([both, both], axis=0)
        for q in range(cap):
            slot = q * n_cols + o
            product = jnp.dot(weight[o, q], both, preferred_element_type=jnp.float32)
            product = product[:, :LANES] + product[:, LANES:]
            product = product.reshape(CORES, tile // ROWS, ROWS, LANES)
            for c in range(CORES):
                target = meta[c, slot]
                for j in range(n_local):
                    add = jnp.where((target == float(j))[None], product[c], 0.0)
                    totals[g, s, c, j] += add.reshape(tile, LANES)

    def place(turn):
        return nearest(turn % size_z, at_z, size_z), nearest(turn // size_z, at_x, size_x)

    def consume(g, s, turn):
        sz, sx = place(turn)
        for part in range(CORES):
            o = (sz * size_x + sx) * CORES + part
            if g == 0 and s == 0:
                build(o)
            multiply(g, s, o)

    def relay_ahead(g, s):
        if turned:
            for ux in range(1, size_x):
                relay(g, s, at_z, nearest(ux, at_x, size_x), CORES - 1, spread=True)

    def relay_x(g, s, turn):
        sz, sx = place(turn)
        for part in range(CORES):
            waited = by_row(part) & (turn % size_z == 0)
            pl.when(jnp.logical_not(waited))(lambda: relay(g, s, sz, sx, part))

    def relay_z(g, s, turn):
        sz, sx = place(turn)
        for part in range(CORES):
            relay(g, s, sz, sx, part)

    def x_turns(g, s):
        @pl.loop(size_z, chips - 1)
        def _(turn):
            relay_x(g, s, turn)
            consume(g, s, turn - 1)

    def fold(g, s):
        for c in range(CORES):
            for r in range(n_rows):
                sums = [totals[g, s, c, r * per + b] for b in range(per)]
                packed[g, s, c, r] = lanes_of(*[value + roll(value) for value in sums])

    def y_copy(s, c, step):
        target = (row + step) % n_rows
        return pltpu.make_async_remote_copy(
            packed.at[0, s, c, target], partner.at[s, c, row], y_send.at[s, c, step - 1], y_recv.at[s, c, step - 1],
            device_id=(target, col), device_id_type=MESH)

    def y_sum(s, c):
        total = packed[0, s, c, row]
        for step in range(1, n_rows):
            origin = (row + n_rows - step) % n_rows
            pltpu.make_async_remote_copy(
                packed.at[0, s, c, row], partner.at[s, c, origin], y_send.at[s, c, step - 1], y_recv.at[s, c, step - 1],
                device_id=(row, col), device_id_type=MESH).wait_recv()
            total = total + partner[s, c, origin]
        return total

    def fin_copies(s):
        copies = []
        for away in range(CORES):
            c = (core + away) % CORES
            for step in range(n_rows):
                if away or step:
                    target = (row + step) % n_rows
                    i = away * n_rows + step
                    copies.append(pltpu.make_async_remote_copy(
                        packed.at[1, s, c, target], final.at[s, away, row], fin_send.at[s, i], fin_recv.at[s, i],
                        device_id=(target, chip * CORES + c), device_id_type=MESH))
        return copies

    def fin_sum(s, away):
        total = None if away else packed[1, s, core, row]
        for step in range(n_rows):
            if away or step:
                origin = (row + n_rows - step) % n_rows
                i = away * n_rows + step
                pltpu.make_async_remote_copy(
                    packed.at[1, s, core, row], final.at[s, away, origin], fin_send.at[s, i], fin_recv.at[s, i],
                    device_id=(row, col), device_id_type=MESH).wait_recv()
                piece = final[s, away, origin]
                total = piece if total is None else total + piece
        return total

    def close(g, s):
        consume(g, s, chips - 1)
        fold(g, s)
        copies = fin_copies(s) if g else [y_copy(s, c, step) for c in range(CORES) for step in range(1, n_rows)]
        for copy in copies:
            copy.start()
        return copies

    def stats_begin(i, rows):
        filler = jnp.zeros((ROWS - len(rows), LANES), jnp.float32)
        stat_col[i, chip] = jnp.concatenate(list(rows) + [filler], axis=0)

        @pl.loop(1, chips)
        def _(step):
            pltpu.make_async_remote_copy(
                stat_col.at[i, chip], stat_col.at[i, chip], col_send.at[i], col_recv.at[i],
                device_id=(row, (chip + step) % chips * CORES + core), device_id_type=MESH).start()

    def stats_turn(i):
        many = stat_col.at[i, pl.ds(0, chips - 1)]
        pltpu.make_async_copy(many, many, col_recv.at[i]).wait()
        stat_row[i, row] = jnp.sum(stat_col[i], axis=0)

        @pl.loop(1, n_rows)
        def _(step):
            pltpu.make_async_remote_copy(
                stat_row.at[i, row], stat_row.at[i, row], row_send.at[i], row_recv.at[i],
                device_id=((row + step) % n_rows, col), device_id_type=MESH).start()

    def stats_end(i):
        many = stat_row.at[i, pl.ds(0, n_rows - 1)]
        pltpu.make_async_copy(many, many, row_recv.at[i]).wait()
        value = jnp.sum(stat_row[i], axis=0)
        return value + roll(value)

    def stats_drain(i):
        many = stat_col.at[i, pl.ds(0, chips - 1)]
        pltpu.make_async_copy(many, many, col_send.at[i]).wait()
        many = stat_row.at[i, pl.ds(0, n_rows - 1)]
        pltpu.make_async_copy(many, many, row_send.at[i]).wait()

    def over_rows(value):
        return jnp.sum(value, axis=0, keepdims=True)

    def pack_own(part):
        units = pack(*[raw[part, b] for b in range(per)])
        for s in range(PARTS):
            held[at_unit(0, s, chip * CORES + part)] = units[s]
        branches(0, 0, at_z, at_x, part)

    for copy in swaps[:per]:
        copy.start()
    for copy in own:
        copy.wait()
    pack_own(core)
    for copy in swaps[per:]:
        copy.start()
    for copy in swaps[:per]:
        copy.wait_recv()
    pack_own(1 - core)
    squares = []
    for s in range(PARTS):
        units = [held[at_unit(0, s, chip * CORES + c)] for c in range(CORES)]
        squares.append(sum(over_rows(unit * unit) for unit in units))
    stats_begin(0, squares)
    swaps[per].wait_recv()
    for c in range(CORES):
        columns = [jnp.broadcast_to(meta[c, slots, pl.ds(b, 1)], (tile, LANES)).T for b in range(per)]
        diag[c] = lanes_of(*columns)

    def open_first():
        for part in range(CORES):
            branches(0, 1, at_z, at_x, part)
        for copy in kept:
            copy.wait()
        swaps[per + 1].wait_recv()

    def gather(g, open_second, hooks):
        relay_z(g, 0, 1)
        relay_ahead(g, 0)
        open_second()
        @pl.loop(2, size_z)
        def _(turn):
            relay_z(g, 0, turn)
            consume(g, 0, turn - 2)
        relay_ahead(g, 1)
        consume(g, 0, size_z - 2)
        @pl.loop(1, size_z - 1)
        def _(turn):
            relay_z(g, 1, turn)
            consume(g, 1, turn - 1)
        hooks[0]()
        x_turns(g, 0)
        relay_x(g, 0, chips - 1)
        consume(g, 0, chips - 2)
        sent = close(g, 0)
        relay_z(g, 1, size_z - 1)
        consume(g, 1, size_z - 2)
        hooks[1]()
        x_turns(g, 1)
        hooks[2]()
        relay_x(g, 1, chips - 1)
        consume(g, 1, chips - 2)
        sent = sent + close(g, 1)
        return sent

    known = {}

    def nothing():
        pass

    def end_first_stats():
        stats = stats_end(0)
        known["squares"] = [stats[s:s + 1] for s in range(PARTS)]
        known["magnitude"] = [jnp.sqrt(stats[s:s + 1] / total_rows + 1e-06) for s in range(PARTS)]
        known["rows"] = []

    def make_image(s):
        image_squares, crossed = 0.0, 0.0
        magnitude = known["magnitude"][s]
        for c in range(CORES):
            unit = held[at_unit(0, s, chip * CORES + c)]
            image = (diag[c] * unit + y_sum(s, c)) / magnitude
            held[at_unit(1, s, chip * CORES + c)] = image
            branches(1, s, at_z, at_x, c)
            image_squares += over_rows(image * image)
            crossed += over_rows(image * (unit / magnitude))
        known["rows"] += [image_squares, crossed]
        to_mate(s).start()

    def to_mate(s):
        return pltpu.make_async_remote_copy(
            held.at[at_unit(1, s, mate)], cross.at[s], cross_send.at[s], cross_recv.at[s],
            device_id=(row, mate), device_id_type=MESH)

    y_sent = gather(0, open_first, (lambda: stats_turn(0), end_first_stats, lambda: make_image(0)))

    to_side = pltpu.make_async_remote_copy(
        side.at[core], side.at[core], side_sem.at[0], side_sem.at[1], device_id=(row, mate), device_id_type=MESH)

    def open_image():
        make_image(1)
        stats_begin(1, known["rows"])

    def end_second_stats():
        stats = stats_end(1)
        rows = []
        for s in range(PARTS):
            image_squares, crossed = stats[2 * s:2 * s + 1], stats[2 * s + 1:2 * s + 2]
            magnitude = known["magnitude"][s]
            basis_squares = known["squares"][s] / (magnitude * magnitude)
            projection = crossed / total_rows
            power = (image_squares - 2.0 * projection * crossed + projection * projection * basis_squares) / total_rows
            rows.append((projection, jnp.sqrt(jnp.maximum(power, 0.0) + 1e-06), magnitude))
        rows = [lanes_of(first, second) for first, second in zip(*rows)]
        side[core] = jnp.concatenate(rows + [jnp.zeros((ROWS - len(rows), LANES), jnp.float32)], axis=0)
        to_side.start()

    places = ((0, mine_at), (1, other_at))

    def image_of(s, away):
        return cross[s] if away else held[at_unit(1, s, col)]

    def make_next():
        to_side.wait_recv()
        for s in range(PARTS):
            to_mate(s).wait_recv()
        for away, at in places:
            values = side[(core + away) % CORES]
            projection, norm_new, magnitude = values[:1], values[1:2], values[2:3]
            images = pack(*[image_of(s, away) for s in range(PARTS)])
            for b in range(per):
                vector = own_other[b] if away else raw[core, b]
                basis = vector / magnitude
                next_ref[pl.ds(b * tile, tile), at] = (images[b] - projection * basis) / norm_new
            column_ref[:, at] = values[:2]

    def finish(s):
        for away, _ in places:
            values = side[(core + away) % CORES]
            values = lanes_of(values, roll(values)) if s == 0 else lanes_of(roll(values), values)
            image = image_of(s, away)
            result[s, away] = (diag[core] * image + fin_sum(s, away) - values[:1] * image) / values[1:2]

    sent = gather(1, open_image, (lambda: stats_turn(1), end_second_stats, make_next))

    finish(0)
    drain_units()
    for g in range(2):
        stats_drain(g)
    for copy in swaps + y_sent + [to_mate(s) for s in range(PARTS)] + [to_side]:
        copy.wait_send()
    finish(1)
    for away, at in places:
        values = pack(*[result[s, away] for s in range(PARTS)])
        for b in range(per):
            second_ref[pl.ds(b * tile, tile), at] = values[b]
    for copy in sent:
        copy.wait_send()


def per_device(blocks, block_row, block_col, counts, diagonal, vector):
    n_rows, n_cols = lax.axis_size("row"), lax.axis_size("col")
    slots, tile, _ = blocks.shape
    mine, rhs = vector.shape
    per = mine // tile
    if rhs != CORES * LANES or tile != LANES or per != PARTS:
        raise ValueError("shapes")
    cap, chips = slots // n_cols, n_cols // CORES
    smem = pl.BlockSpec(memory_space=pltpu.SMEM)
    vmem = pl.BlockSpec(memory_space=pltpu.VMEM)
    anywhere = pl.BlockSpec(memory_space=pl.ANY)
    f32, dma = jnp.float32, pltpu.SemaphoreType.DMA
    unit = (tile, LANES)
    return pl.pallas_call(
        functools.partial(kernel, n_rows, n_cols, mine * n_rows * n_cols),
        out_shape=(
            jax.ShapeDtypeStruct((mine, rhs), f32),
            jax.ShapeDtypeStruct((mine, rhs), f32),
            jax.ShapeDtypeStruct((2, rhs), f32),
        ),
        in_specs=[smem, smem, smem, anywhere, vmem, anywhere],
        out_specs=(vmem, vmem, vmem),
        scratch_shapes=[
            pltpu.VMEM((CORES, slots, tile, tile), f32),
            pltpu.VMEM((2 * PARTS * n_cols,) + unit, f32),
            pltpu.VMEM((n_cols, cap, CORES * tile, 2 * tile), jnp.bfloat16),
            pltpu.VMEM((2, PARTS, CORES, n_rows * per) + unit, f32),
            pltpu.VMEM((2, PARTS, CORES, n_rows) + unit, f32),
            pltpu.VMEM((PARTS, CORES, n_rows) + unit, f32),
            pltpu.VMEM((PARTS, CORES, n_rows) + unit, f32),
            pltpu.VMEM((CORES,) + unit, f32),
            pltpu.VMEM((CORES, slots + 1, ROWS, LANES), f32),
            pltpu.VMEM((CORES, per) + unit, f32),
            pltpu.VMEM((per,) + unit, f32),
            pltpu.VMEM((PARTS,) + unit, f32),
            pltpu.VMEM((PARTS, CORES) + unit, f32),
            pltpu.VMEM((CORES, ROWS, LANES), f32),
            pltpu.VMEM((2, chips, ROWS, LANES), f32),
            pltpu.VMEM((2, n_rows, ROWS, LANES), f32),
            dma((2 * per + 1,)),
            dma((per + 2,)), dma((per + 2,)),
            dma((4,)), dma((2 * PARTS * n_cols,)),
            dma((PARTS, CORES, n_rows - 1)), dma((PARTS, CORES, n_rows - 1)),
            dma((PARTS, CORES * n_rows)), dma((PARTS, CORES * n_rows)),
            dma((PARTS,)), dma((PARTS,)), dma((2,)),
            dma((2,)), dma((2,)), dma((2,)), dma((2,)),
        ],
        compiler_params=pltpu.CompilerParams(
            collective_id=0, has_side_effects=True, vmem_limit_bytes=60 * 1024 * 1024),
    )(block_row, block_col, counts, blocks, diagonal.reshape(per, tile), vector)


def solution(mesh):
    spec = P(("row", "col"))
    return jax.shard_map(
        per_device,
        mesh=mesh,
        in_specs=(P(("row", "col"), None, None), spec, spec, spec, spec, P(("row", "col"), None)),
        out_specs=(P(("row", "col"), None), P(("row", "col"), None), P()),
        check_vma=False,
    )
```

```python
import functools

import jax
import jax.numpy as jnp
from jax import lax
from jax.experimental import pallas as pl
from jax.experimental.pallas import tpu as pltpu
from jax.sharding import PartitionSpec as P

MESH = pl.DeviceIdType.MESH
LANES = 128
ROWS = 8
CORES = 2
HALF = LANES // 2
PARTS = LANES // HALF


def chip_grid(chips):
    x = max(d for d in range(1, chips + 1) if chips % d == 0 and d * d <= chips)
    return chips // x, x


def nearest(turn, here, size):
    both = jnp.minimum(here, size - 1 - here)
    reach = (turn + 1) // 2
    near = jnp.where(turn % 2 == 1, here + reach, here - reach)
    far = jnp.where(here < size - 1 - here, turn, size - 1 - turn)
    return jnp.where(turn <= 2 * both, near, far)


def split(value):
    high = value.astype(jnp.bfloat16)
    low = (value - high.astype(jnp.float32)).astype(jnp.bfloat16)
    return high, low


def roll(value):
    return pltpu.roll(value, HALF, 1)


FIRST, SECOND = (
    (
        ("own", 0, 0), ("beside", 0, 0), ("z", 0, 1), ("z", 0, 2), ("z", 0, 3), ("x", 0, 0),
        ("z", 1, 1), ("x", 0, 2), ("x", 0, 1), ("z", 1, 2), ("beside", 1, 0), ("x", 1, 0),
        ("x", 0, 3), ("close", 0, 0), ("z", 1, 3), ("image", 0, 0), ("x", 1, 1), ("x", 1, 2),
        ("x", 1, 3), ("close", 1, 0),
    ),
    (
        ("own", 0, 0), ("beside", 0, 0), ("z", 0, 1), ("z", 0, 2), ("z", 0, 3), ("x", 0, 0),
        ("z", 1, 1), ("x", 0, 2), ("x", 0, 1), ("z", 1, 2), ("beside", 1, 0), ("x", 1, 0),
        ("x", 0, 3), ("close", 0, 0), ("z", 1, 3), ("x", 1, 1), ("x", 1, 2), ("x", 1, 3),
        ("close", 1, 0),
    ),
)


def order(g, size_z):
    if size_z == 4:
        return (FIRST, SECOND)[g]
    steps = [("own", 0, 0)]
    for s in range(PARTS):
        steps += [("beside", s, 0)] + [("z", s, t) for t in range(1, size_z)]
        steps += [("x", s, t) for t in range(size_z)] + [("close", s, 0)]
    return steps if g else steps[:-1] + [("image", 0, 0), steps[-1]]


def kernel(
    n_rows, n_cols, total_rows,
    brow_hbm, bcol_hbm, counts_hbm, blocks_hbm, diag_hbm, vec_hbm,
    next_ref, second_ref, column_ref,
    brow, bcol, counts, diag_ref, blocks, held, weight, totals, packed, partner, final, diag, meta, raw, other_units, own_other, cross, result, side,
    stat_col, stat_row,
    local_sem, small_sem, mate_send, swap_send, swap_recv, unit_send, unit_recv, y_send, y_recv, fin_send, fin_recv,
    cross_send, cross_recv, side_sem, col_send, col_recv, row_send, row_recv,
):
    slots, tile = blocks.shape[1], blocks.shape[2]
    cap = slots // n_cols
    per = raw.shape[0]
    n_local = n_rows * per
    chips = n_cols // CORES
    size_z, size_x = chip_grid(chips)
    row, col = lax.axis_index("row"), lax.axis_index("col")
    core, chip = col % CORES, col // CORES
    mate = chip * CORES + 1 - core
    at_x, at_z = chip % size_x, chip // size_x
    mine_at = pl.ds(pl.multiple_of(core * LANES, LANES), LANES)
    other_at = pl.ds(pl.multiple_of((1 - core) * LANES, LANES), LANES)
    low_lane = lax.broadcasted_iota(jnp.int32, (ROWS, LANES), 1) < HALF
    low_row = low_lane[:1]

    own = []
    for b in range(per):
        at = pl.ds(b * tile, tile)
        own.append(pltpu.make_async_copy(vec_hbm.at[at, mine_at], raw.at[b], local_sem.at[b]))
        own.append(pltpu.make_async_copy(vec_hbm.at[at, other_at], own_other.at[b], local_sem.at[per + b]))
    own_blocks = pltpu.make_async_copy(blocks_hbm, blocks.at[core], local_sem.at[2 * per])
    small = [
        pltpu.make_async_copy(source, target, small_sem.at[i]) for i, (source, target) in enumerate(
            ((brow_hbm, brow), (bcol_hbm, bcol), (counts_hbm, counts), (diag_hbm, diag_ref)))]
    for copy in own + small + [own_blocks]:
        copy.start()

    barrier = pltpu.get_barrier_semaphore()

    @pl.loop(1, n_cols)
    def _(step):
        pl.semaphore_signal(barrier, inc=1, device_id=(row, (col + step) % n_cols), device_id_type=MESH)

    @pl.loop(1, n_rows)
    def _(step):
        there = (row + step) % n_rows
        pl.semaphore_signal(barrier, inc=1, device_id=(there, col), device_id_type=MESH)
        pl.semaphore_signal(barrier, inc=1, device_id=(there, mate), device_id_type=MESH)

    pl.semaphore_wait(barrier, n_cols - 1 + 2 * (n_rows - 1))

    swaps = []

    def swap(source, target):
        i = len(swaps)
        swaps.append(pltpu.make_async_remote_copy(
            source, target, swap_send.at[i], swap_recv.at[i], device_id=(row, mate), device_id_type=MESH))

    swap(meta.at[core], meta.at[core])
    swap(blocks_hbm, blocks.at[core])

    def lanes_of(low, high):
        keep = low_row if low.shape[0] == 1 else low_lane
        shape = low.shape
        low, high = low.reshape((-1,) + keep.shape), high.reshape((-1,) + keep.shape)
        return jnp.where(keep[None], low, high).reshape(shape)

    def pack(first, second):
        return lanes_of(first, roll(second)), lanes_of(roll(first), second)

    def at_unit(g, s, o):
        return (g * PARTS + s) * n_cols + o

    turned = size_x > 1 and size_z % 2 == 0

    def beside(z):
        return z + 1 - 2 * (z % 2)

    def by_row(part):
        return (part == CORES - 1) if turned else (part < 0)

    def branches(g, s, sz, sx, part, spread=False, source=None):
        o = (sz * size_x + sx) * CORES + part
        there = core if source is None else 1 - core
        along_z = at_x == sx
        along_x = jnp.logical_not(by_row(part) & (sz == beside(at_z)))
        targets = [
            (0, along_z & (at_z >= sz) & (at_z + 1 < size_z), at_x, at_z + 1),
            (1, along_z & (at_z <= sz) & (at_z >= 1), at_x, at_z - 1),
            (2, along_x & (at_x >= sx) & (at_x + 1 < size_x), at_x + 1, at_z),
            (3, along_x & (at_x <= sx) & (at_x >= 1), at_x - 1, at_z),
        ]
        if spread:
            targets = targets[2:]
            targets += [(0, at_z % 2 == 0, at_x, at_z + 1), (1, at_z % 2 == 1, at_x, at_z - 1)]
        piece = held.at[at_unit(g, s, o)]
        source = piece if source is None else source
        for i, wanted, tx, tz in targets:
            def go(i=i, tx=tx, tz=tz):
                pltpu.make_async_remote_copy(
                    source, piece, unit_send.at[i], unit_recv.at[at_unit(g, s, o)],
                    device_id=(row, (tz * size_x + tx) * CORES + there), device_id_type=MESH).start()
            pl.when(wanted)(go)

    def drain_units():
        extra = size_x - 1 if turned else 0

        def wait(i, n, wanted):
            def go():
                many = held.at[pl.ds(0, 2 * PARTS * n)]
                pltpu.make_async_copy(many, many, unit_send.at[i]).wait()
            pl.when(wanted)(go)

        for v in range(size_z):
            if v + 1 < size_z:
                wait(0, (v + 1) * CORES + (extra if v % 2 == 0 else 0), at_z == v)
            if v:
                wait(1, (size_z - v) * CORES + (extra if v % 2 else 0), at_z == v)
        for v in range(size_x - 1):
            n = (v + 1) * (CORES * size_z - (1 if turned else 0))
            wait(2, n, at_x == v)
            wait(3, n, at_x == size_x - 1 - v)

    def relay(g, s, sz, sx, part, spread=False):
        unit = at_unit(g, s, (sz * size_x + sx) * CORES + part)
        piece = held.at[unit]
        pltpu.make_async_remote_copy(
            piece, piece, unit_send.at[0], unit_recv.at[unit],
            device_id=(row, col), device_id_type=MESH).wait_recv()
        branches(g, s, sz, sx, part, spread)

    def build(o):
        for q in range(cap):
            slot = q * n_cols + o
            for c in range(CORES):
                high, low = split(blocks[c, slot].T)
                weight[o, q, pl.ds(c * tile, tile), pl.ds(0, tile)] = high
                weight[o, q, pl.ds(c * tile, tile), pl.ds(tile, tile)] = low

    def multiply(g, s, o):
        both = jnp.concatenate(split(held[at_unit(g, s, o)]), axis=1)
        both = jnp.concatenate([both, both], axis=0)
        for q in range(cap):
            slot = q * n_cols + o
            product = jnp.dot(weight[o, q], both, preferred_element_type=jnp.float32)
            product = product[:, :LANES] + product[:, LANES:]
            product = product.reshape(CORES, tile // ROWS, ROWS, LANES)
            for c in range(CORES):
                target = meta[c, slot]
                for j in range(n_local):
                    add = jnp.where((target == float(j))[None], product[c], 0.0)
                    totals[g, s, c, j] += add.reshape(tile, LANES)

    def place(turn):
        return nearest(turn % size_z, at_z, size_z), nearest(turn // size_z, at_x, size_x)

    def consume(g, s, turn):
        sz, sx = place(turn)
        for part in range(CORES):
            o = (sz * size_x + sx) * CORES + part
            if g == 0 and s == 0:
                build(o)
            multiply(g, s, o)

    def relay_ahead(g, s):
        if turned:
            for ux in range(1, size_x):
                relay(g, s, at_z, nearest(ux, at_x, size_x), CORES - 1, spread=True)

    def relay_x(g, s, turn):
        sz, sx = place(turn)
        for part in range(CORES):
            waited = by_row(part) & (turn % size_z == 0)
            pl.when(jnp.logical_not(waited))(lambda: relay(g, s, sz, sx, part))

    def relay_z(g, s, turn):
        sz, sx = place(turn)
        for part in range(CORES):
            relay(g, s, sz, sx, part)

    def x_turns(g, s):
        @pl.loop(size_z, chips - 1)
        def _(turn):
            relay_x(g, s, turn)
            consume(g, s, turn - 1)

    def fold(g, s):
        for c in range(CORES):
            for r in range(n_rows):
                sums = [totals[g, s, c, r * per + b] for b in range(per)]
                packed[g, s, c, r] = lanes_of(*[value + roll(value) for value in sums])

    def y_copy(s, c, step):
        target = (row + step) % n_rows
        return pltpu.make_async_remote_copy(
            packed.at[0, s, c, target], partner.at[s, c, row], y_send.at[s, c, step - 1], y_recv.at[s, c, step - 1],
            device_id=(target, col), device_id_type=MESH)

    def y_sum(s, c):
        total = packed[0, s, c, row]
        for step in range(1, n_rows):
            origin = (row + n_rows - step) % n_rows
            pltpu.make_async_remote_copy(
                packed.at[0, s, c, row], partner.at[s, c, origin], y_send.at[s, c, step - 1], y_recv.at[s, c, step - 1],
                device_id=(row, col), device_id_type=MESH).wait_recv()
            total = total + partner[s, c, origin]
        return total

    def fin_copies(s):
        copies = []
        for away in range(CORES):
            c = (core + away) % CORES
            for step in range(n_rows):
                if away or step:
                    target = (row + step) % n_rows
                    i = away * n_rows + step
                    copies.append(pltpu.make_async_remote_copy(
                        packed.at[1, s, c, target], final.at[s, away, row], fin_send.at[s, i], fin_recv.at[s, i],
                        device_id=(target, chip * CORES + c), device_id_type=MESH))
        return copies

    def fin_sum(s, away):
        total = None if away else packed[1, s, core, row]
        for step in range(n_rows):
            if away or step:
                origin = (row + n_rows - step) % n_rows
                i = away * n_rows + step
                pltpu.make_async_remote_copy(
                    packed.at[1, s, core, row], final.at[s, away, origin], fin_send.at[s, i], fin_recv.at[s, i],
                    device_id=(row, col), device_id_type=MESH).wait_recv()
                piece = final[s, away, origin]
                total = piece if total is None else total + piece
        return total

    def close(g, s):
        fold(g, s)
        copies = fin_copies(s) if g else [y_copy(s, c, step) for c in range(CORES) for step in range(1, n_rows)]
        for copy in copies:
            copy.start()
        return copies

    def stats_begin(i, rows):
        filler = jnp.zeros((ROWS - len(rows), LANES), jnp.float32)
        stat_col[i, chip] = jnp.concatenate(list(rows) + [filler], axis=0)

        @pl.loop(1, chips)
        def _(step):
            pltpu.make_async_remote_copy(
                stat_col.at[i, chip], stat_col.at[i, chip], col_send.at[i], col_recv.at[i],
                device_id=(row, (chip + step) % chips * CORES + core), device_id_type=MESH).start()

    def stats_turn(i):
        many = stat_col.at[i, pl.ds(0, chips - 1)]
        pltpu.make_async_copy(many, many, col_recv.at[i]).wait()
        stat_row[i, row] = jnp.sum(stat_col[i], axis=0)

        @pl.loop(1, n_rows)
        def _(step):
            pltpu.make_async_remote_copy(
                stat_row.at[i, row], stat_row.at[i, row], row_send.at[i], row_recv.at[i],
                device_id=((row + step) % n_rows, col), device_id_type=MESH).start()

    def stats_end(i):
        many = stat_row.at[i, pl.ds(0, n_rows - 1)]
        pltpu.make_async_copy(many, many, row_recv.at[i]).wait()
        value = jnp.sum(stat_row[i], axis=0)
        return value + roll(value)

    def stats_drain(i):
        many = stat_col.at[i, pl.ds(0, chips - 1)]
        pltpu.make_async_copy(many, many, col_send.at[i]).wait()
        many = stat_row.at[i, pl.ds(0, n_rows - 1)]
        pltpu.make_async_copy(many, many, row_send.at[i]).wait()

    def over_rows(value):
        return jnp.sum(value, axis=0, keepdims=True)

    def own_units(s):
        branches(0, s, at_z, at_x, core)
        branches(0, s, at_z, at_x, core, source=other_units.at[s])

    def unit_to_mate(s):
        return pltpu.make_async_remote_copy(
            other_units.at[s], held.at[at_unit(0, s, col)], mate_send.at[s], unit_recv.at[at_unit(0, s, col)],
            device_id=(row, mate), device_id_type=MESH)

    def unit_from_mate(s):
        unit = held.at[at_unit(0, s, mate)]
        pltpu.make_async_remote_copy(
            unit, unit, mate_send.at[s], unit_recv.at[at_unit(0, s, mate)],
            device_id=(row, mate), device_id_type=MESH).wait_recv()

    for copy in own:
        copy.wait()
    mine_packed = pack(*[raw[b] for b in range(per)])
    other_packed = pack(*[own_other[b] for b in range(per)])
    for s in range(PARTS):
        held[at_unit(0, s, col)] = mine_packed[s]
        other_units[s] = other_packed[s]
        if s == 0:
            own_units(0)
    for s in range(PARTS):
        unit_to_mate(s).start()
    for copy in small:
        copy.wait()
    @pl.loop(0, slots)
    def _(slot):
        piece = bcol[slot] // per
        target = piece // n_cols * per + bcol[slot] % per
        target = jnp.where(slot < counts[0], target, -1)
        reads_low = jnp.where(low_lane, 0, 1) == brow[slot] % per
        meta[core, slot] = jnp.where(reads_low, target, -1).astype(jnp.float32)

    filler = jnp.zeros((ROWS - per, LANES), jnp.float32)
    meta[core, slots] = jnp.concatenate([diag_ref[...], filler], axis=0)
    totals[...] = jnp.zeros_like(totals)
    for copy in swaps:
        copy.start()
    for s in range(PARTS):
        unit_from_mate(s)
    squares = []
    for s in range(PARTS):
        units = [held[at_unit(0, s, chip * CORES + c)] for c in range(CORES)]
        squares.append(sum(over_rows(unit * unit) for unit in units))
    stats_begin(0, squares)
    swaps[0].wait_recv()
    for c in range(CORES):
        columns = [jnp.broadcast_to(meta[c, slots, pl.ds(b, 1)], (tile, LANES)).T for b in range(per)]
        diag[c] = lanes_of(*columns)

    def open_first():
        own_units(1)
        own_blocks.wait()
        swaps[1].wait_recv()

    middle = (at_z > 0) & (at_z + 1 < size_z)

    def gather(g, open_second, hooks):
        sent, halfway = [], []
        waiting = [[0] for _ in range(PARTS)]
        turned_stats = False
        for what, s, turn in order(g, size_z):
            if what[0] == "z" and s and not turned_stats:
                stats_turn(g)
                turned_stats = True
            if what == "own":
                open_second()
            elif what == "beside":
                relay_ahead(g, s)
            elif what == "image":
                hooks[2]()
            elif what == "close":
                for ready in waiting[s]:
                    consume(g, s, ready)
                sent += close(g, s)
                waiting[s] = []
                hooks[s]()
            else:
                came = [turn]
                if what == "z":
                    relay_z(g, s, turn)
                elif what == "x":
                    came = [turn + ux * size_z for ux in range(1, size_x)]
                    for other in came:
                        relay_x(g, s, other)
                else:
                    wanted = middle if what == "zm" else jnp.logical_not(middle)
                    pl.when(wanted)(lambda: relay_z(g, s, turn))
                    if (s, turn) not in halfway:
                        halfway.append((s, turn))
                        came = []
                for h in range(PARTS):
                    for ready in waiting[h]:
                        consume(g, h, ready)
                    waiting[h] = []
                waiting[s] += came
        return sent

    known = {}

    def nothing():
        pass

    def end_first_stats():
        stats = stats_end(0)
        known["squares"] = [stats[s:s + 1] for s in range(PARTS)]
        known["magnitude"] = [jnp.sqrt(stats[s:s + 1] / total_rows + 1e-06) for s in range(PARTS)]
        known["rows"] = []

    def make_image(s):
        image_squares, crossed = 0.0, 0.0
        magnitude = known["magnitude"][s]
        for c in range(CORES):
            unit = held[at_unit(0, s, chip * CORES + c)]
            image = (diag[c] * unit + y_sum(s, c)) / magnitude
            held[at_unit(1, s, chip * CORES + c)] = image
            branches(1, s, at_z, at_x, c)
            image_squares += over_rows(image * image)
            crossed += over_rows(image * (unit / magnitude))
        known["rows"] += [image_squares, crossed]
        to_mate(s).start()

    def to_mate(s):
        return pltpu.make_async_remote_copy(
            held.at[at_unit(1, s, mate)], cross.at[s], cross_send.at[s], cross_recv.at[s],
            device_id=(row, mate), device_id_type=MESH)

    y_sent = gather(0, open_first, (end_first_stats, nothing, lambda: make_image(0)))

    to_side = pltpu.make_async_remote_copy(
        side.at[core], side.at[core], side_sem.at[0], side_sem.at[1], device_id=(row, mate), device_id_type=MESH)

    def open_image():
        make_image(1)
        stats_begin(1, known["rows"])

    def end_second_stats():
        stats = stats_end(1)
        rows = []
        for s in range(PARTS):
            image_squares, crossed = stats[2 * s:2 * s + 1], stats[2 * s + 1:2 * s + 2]
            magnitude = known["magnitude"][s]
            basis_squares = known["squares"][s] / (magnitude * magnitude)
            projection = crossed / total_rows
            power = (image_squares - 2.0 * projection * crossed + projection * projection * basis_squares) / total_rows
            rows.append((projection, jnp.sqrt(jnp.maximum(power, 0.0) + 1e-06), magnitude))
        rows = [lanes_of(first, second) for first, second in zip(*rows)]
        side[core] = jnp.concatenate(rows + [jnp.zeros((ROWS - len(rows), LANES), jnp.float32)], axis=0)
        to_side.start()

    places = ((0, mine_at), (1, other_at))

    def image_of(s, away):
        return cross[s] if away else held[at_unit(1, s, col)]

    def make_next():
        to_side.wait_recv()
        for s in range(PARTS):
            to_mate(s).wait_recv()
        for away, at in places:
            values = side[(core + away) % CORES]
            projection, norm_new, magnitude = values[:1], values[1:2], values[2:3]
            images = pack(*[image_of(s, away) for s in range(PARTS)])
            for b in range(per):
                vector = own_other[b] if away else raw[b]
                basis = vector / magnitude
                next_ref[pl.ds(b * tile, tile), at] = (images[b] - projection * basis) / norm_new
            column_ref[:, at] = values[:2]

    def finish(s):
        for away, _ in places:
            values = side[(core + away) % CORES]
            values = lanes_of(values, roll(values)) if s == 0 else lanes_of(roll(values), values)
            image = image_of(s, away)
            result[s, away] = (diag[core] * image + fin_sum(s, away) - values[:1] * image) / values[1:2]

    sent = gather(1, open_image, (end_second_stats, make_next, nothing))

    finish(0)
    drain_units()
    for g in range(2):
        stats_drain(g)
    for copy in swaps + y_sent + [move(s) for move in (unit_to_mate, to_mate) for s in range(PARTS)] + [to_side]:
        copy.wait_send()
    finish(1)
    for away, at in places:
        values = pack(*[result[s, away] for s in range(PARTS)])
        for b in range(per):
            second_ref[pl.ds(b * tile, tile), at] = values[b]
    for copy in sent:
        copy.wait_send()


def per_device(blocks, block_row, block_col, counts, diagonal, vector):
    n_rows, n_cols = lax.axis_size("row"), lax.axis_size("col")
    slots, tile, _ = blocks.shape
    mine, rhs = vector.shape
    per = mine // tile
    if rhs != CORES * LANES or tile != LANES or per != PARTS:
        raise ValueError("shapes")
    cap, chips = slots // n_cols, n_cols // CORES
    vmem = pl.BlockSpec(memory_space=pltpu.VMEM)
    anywhere = pl.BlockSpec(memory_space=pl.ANY)
    f32, dma = jnp.float32, pltpu.SemaphoreType.DMA
    unit = (tile, LANES)
    return pl.pallas_call(
        functools.partial(kernel, n_rows, n_cols, mine * n_rows * n_cols),
        out_shape=(
            jax.ShapeDtypeStruct((mine, rhs), f32),
            jax.ShapeDtypeStruct((mine, rhs), f32),
            jax.ShapeDtypeStruct((2, rhs), f32),
        ),
        in_specs=[anywhere] * 6,
        out_specs=(vmem, vmem, vmem),
        scratch_shapes=[
            pltpu.SMEM((slots,), jnp.int32),
            pltpu.SMEM((slots,), jnp.int32),
            pltpu.SMEM((1,), jnp.int32),
            pltpu.VMEM((per, tile), f32),
            pltpu.VMEM((CORES, slots, tile, tile), f32),
            pltpu.VMEM((2 * PARTS * n_cols,) + unit, f32),
            pltpu.VMEM((n_cols, cap, CORES * tile, 2 * tile), jnp.bfloat16),
            pltpu.VMEM((2, PARTS, CORES, n_rows * per) + unit, f32),
            pltpu.VMEM((2, PARTS, CORES, n_rows) + unit, f32),
            pltpu.VMEM((PARTS, CORES, n_rows) + unit, f32),
            pltpu.VMEM((PARTS, CORES, n_rows) + unit, f32),
            pltpu.VMEM((CORES,) + unit, f32),
            pltpu.VMEM((CORES, slots + 1, ROWS, LANES), f32),
            pltpu.VMEM((per,) + unit, f32),
            pltpu.VMEM((PARTS,) + unit, f32),
            pltpu.VMEM((per,) + unit, f32),
            pltpu.VMEM((PARTS,) + unit, f32),
            pltpu.VMEM((PARTS, CORES) + unit, f32),
            pltpu.VMEM((CORES, ROWS, LANES), f32),
            pltpu.VMEM((2, chips, ROWS, LANES), f32),
            pltpu.VMEM((2, n_rows, ROWS, LANES), f32),
            dma((2 * per + 1,)), dma((4,)), dma((PARTS,)),
            dma((2,)), dma((2,)),
            dma((4,)), dma((2 * PARTS * n_cols,)),
            dma((PARTS, CORES, n_rows - 1)), dma((PARTS, CORES, n_rows - 1)),
            dma((PARTS, CORES * n_rows)), dma((PARTS, CORES * n_rows)),
            dma((PARTS,)), dma((PARTS,)), dma((2,)),
            dma((2,)), dma((2,)), dma((2,)), dma((2,)),
        ],
        compiler_params=pltpu.CompilerParams(
            collective_id=0, has_side_effects=True, vmem_limit_bytes=60 * 1024 * 1024),
    )(block_row, block_col, counts, blocks, diagonal.reshape(per, tile), vector)


def solution(mesh):
    spec = P(("row", "col"))
    return jax.shard_map(
        per_device,
        mesh=mesh,
        in_specs=(P(("row", "col"), None, None), spec, spec, spec, spec, P(("row", "col"), None)),
        out_specs=(P(("row", "col"), None), P(("row", "col"), None), P()),
        check_vma=False,
    )
```

```python
import functools

import jax
import jax.numpy as jnp
from jax import lax
from jax.experimental import pallas as pl
from jax.experimental.pallas import tpu as pltpu
from jax.sharding import PartitionSpec as P

MESH = pl.DeviceIdType.MESH
LANES = 128
ROWS = 8
CORES = 2
HALF = LANES // 2
PARTS = LANES // HALF


def chip_grid(chips):
    x = max(d for d in range(1, chips + 1) if chips % d == 0 and d * d <= chips)
    return chips // x, x


def nearest(turn, here, size):
    both = jnp.minimum(here, size - 1 - here)
    reach = (turn + 1) // 2
    near = jnp.where(turn % 2 == 1, here + reach, here - reach)
    far = jnp.where(here < size - 1 - here, turn, size - 1 - turn)
    return jnp.where(turn <= 2 * both, near, far)


def split(value):
    high = value.astype(jnp.bfloat16)
    low = (value - high.astype(jnp.float32)).astype(jnp.bfloat16)
    return high, low


def roll(value):
    return pltpu.roll(value, HALF, 1)


FIRST, SECOND = (
    (
        ("own", 0, 0), ("beside", 0, 0), ("z", 0, 1), ("z", 0, 2), ("z", 0, 3), ("x", 0, 0),
        ("z", 1, 1), ("x", 0, 2), ("x", 0, 1), ("z", 1, 2), ("beside", 1, 0), ("x", 1, 0),
        ("x", 0, 3), ("close", 0, 0), ("z", 1, 3), ("image", 0, 0), ("x", 1, 1), ("x", 1, 2),
        ("x", 1, 3), ("close", 1, 0),
    ),
    (
        ("own", 0, 0), ("beside", 0, 0), ("z", 0, 1), ("z", 0, 2), ("z", 0, 3), ("x", 0, 0),
        ("z", 1, 1), ("x", 0, 2), ("x", 0, 1), ("z", 1, 2), ("beside", 1, 0), ("x", 1, 0),
        ("x", 0, 3), ("close", 0, 0), ("z", 1, 3), ("x", 1, 1), ("x", 1, 2), ("x", 1, 3),
        ("close", 1, 0),
    ),
)


def order(g, size_z):
    if size_z == 4:
        return (FIRST, SECOND)[g]
    steps = [("own", 0, 0)]
    for s in range(PARTS):
        steps += [("beside", s, 0)] + [("z", s, t) for t in range(1, size_z)]
        steps += [("x", s, t) for t in range(size_z)] + [("close", s, 0)]
    return steps if g else steps[:-1] + [("image", 0, 0), steps[-1]]


def kernel(
    n_rows, n_cols, total_rows,
    brow_hbm, bcol_hbm, counts_hbm, blocks_hbm, diag_hbm, vec_hbm,
    next_ref, second_ref, column_ref,
    brow, bcol, counts, diag_ref, blocks, held, weight, totals, packed, partner, final, diag, meta, raw, other_units, own_other, cross, result, side,
    stat_col, stat_row,
    local_sem, small_sem, mate_send, swap_send, swap_recv, unit_send, unit_recv, y_send, y_recv, fin_send, fin_recv,
    cross_send, cross_recv, side_sem, col_send, col_recv, row_send, row_recv,
):
    slots, tile = blocks.shape[1], blocks.shape[2]
    cap = slots // n_cols
    per = raw.shape[0]
    n_local = n_rows * per
    chips = n_cols // CORES
    size_z, size_x = chip_grid(chips)
    row, col = lax.axis_index("row"), lax.axis_index("col")
    core, chip = col % CORES, col // CORES
    mate = chip * CORES + 1 - core
    at_x, at_z = chip % size_x, chip // size_x
    mine_at = pl.ds(pl.multiple_of(core * LANES, LANES), LANES)
    other_at = pl.ds(pl.multiple_of((1 - core) * LANES, LANES), LANES)
    low_lane = lax.broadcasted_iota(jnp.int32, (ROWS, LANES), 1) < HALF
    low_row = low_lane[:1]

    own = []
    for b in range(per):
        at = pl.ds(b * tile, tile)
        own.append(pltpu.make_async_copy(vec_hbm.at[at, mine_at], raw.at[b], local_sem.at[b]))
        own.append(pltpu.make_async_copy(vec_hbm.at[at, other_at], own_other.at[b], local_sem.at[per + b]))
    own_blocks = pltpu.make_async_copy(blocks_hbm, blocks.at[core], local_sem.at[2 * per])
    small = [
        pltpu.make_async_copy(source, target, small_sem.at[i]) for i, (source, target) in enumerate(
            ((brow_hbm, brow), (bcol_hbm, bcol), (counts_hbm, counts), (diag_hbm, diag_ref)))]
    for copy in own + small + [own_blocks]:
        copy.start()

    barrier = pltpu.get_barrier_semaphore()

    @pl.loop(1, n_cols)
    def _(step):
        pl.semaphore_signal(barrier, inc=1, device_id=(row, (col + step) % n_cols), device_id_type=MESH)

    @pl.loop(1, n_rows)
    def _(step):
        there = (row + step) % n_rows
        pl.semaphore_signal(barrier, inc=1, device_id=(there, col), device_id_type=MESH)
        pl.semaphore_signal(barrier, inc=1, device_id=(there, mate), device_id_type=MESH)

    pl.semaphore_wait(barrier, n_cols - 1 + 2 * (n_rows - 1))

    swaps = []

    def swap(source, target):
        i = len(swaps)
        swaps.append(pltpu.make_async_remote_copy(
            source, target, swap_send.at[i], swap_recv.at[i], device_id=(row, mate), device_id_type=MESH))

    swap(meta.at[core], meta.at[core])
    swap(blocks_hbm, blocks.at[core])

    def lanes_of(low, high):
        keep = low_row if low.shape[0] == 1 else low_lane
        shape = low.shape
        low, high = low.reshape((-1,) + keep.shape), high.reshape((-1,) + keep.shape)
        return jnp.where(keep[None], low, high).reshape(shape)

    def pack(first, second):
        return lanes_of(first, roll(second)), lanes_of(roll(first), second)

    def at_unit(g, s, o):
        return (g * PARTS + s) * n_cols + o

    turned = size_x > 1 and size_z % 2 == 0

    def beside(z):
        return z + 1 - 2 * (z % 2)

    def by_row(part):
        return (part == CORES - 1) if turned else (part < 0)

    def branches(g, s, sz, sx, part, spread=False, source=None):
        o = (sz * size_x + sx) * CORES + part
        there = core if source is None else 1 - core
        along_z = at_x == sx
        along_x = jnp.logical_not(by_row(part) & (sz == beside(at_z)))
        targets = [
            (0, along_z & (at_z >= sz) & (at_z + 1 < size_z), at_x, at_z + 1),
            (1, along_z & (at_z <= sz) & (at_z >= 1), at_x, at_z - 1),
            (2, along_x & (at_x >= sx) & (at_x + 1 < size_x), at_x + 1, at_z),
            (3, along_x & (at_x <= sx) & (at_x >= 1), at_x - 1, at_z),
        ]
        if spread:
            targets = targets[2:]
            targets += [(0, at_z % 2 == 0, at_x, at_z + 1), (1, at_z % 2 == 1, at_x, at_z - 1)]
        piece = held.at[at_unit(g, s, o)]
        source = piece if source is None else source
        for i, wanted, tx, tz in targets:
            def go(i=i, tx=tx, tz=tz):
                pltpu.make_async_remote_copy(
                    source, piece, unit_send.at[i], unit_recv.at[at_unit(g, s, o)],
                    device_id=(row, (tz * size_x + tx) * CORES + there), device_id_type=MESH).start()
            pl.when(wanted)(go)

    def drain_units():
        extra = size_x - 1 if turned else 0

        def wait(i, n, wanted):
            def go():
                many = held.at[pl.ds(0, 2 * PARTS * n)]
                pltpu.make_async_copy(many, many, unit_send.at[i]).wait()
            pl.when(wanted)(go)

        for v in range(size_z):
            if v + 1 < size_z:
                wait(0, (v + 1) * CORES + (extra if v % 2 == 0 else 0), at_z == v)
            if v:
                wait(1, (size_z - v) * CORES + (extra if v % 2 else 0), at_z == v)
        for v in range(size_x - 1):
            n = (v + 1) * (CORES * size_z - (1 if turned else 0))
            wait(2, n, at_x == v)
            wait(3, n, at_x == size_x - 1 - v)

    def relay(g, s, sz, sx, part, spread=False):
        unit = at_unit(g, s, (sz * size_x + sx) * CORES + part)
        piece = held.at[unit]
        pltpu.make_async_remote_copy(
            piece, piece, unit_send.at[0], unit_recv.at[unit],
            device_id=(row, col), device_id_type=MESH).wait_recv()
        branches(g, s, sz, sx, part, spread)

    def build(o):
        for q in range(cap):
            slot = q * n_cols + o
            for c in range(CORES):
                high, low = split(blocks[c, slot].T)
                weight[o, q, pl.ds(c * tile, tile), pl.ds(0, tile)] = high
                weight[o, q, pl.ds(c * tile, tile), pl.ds(tile, tile)] = low

    def multiply(g, s, o):
        both = jnp.concatenate(split(held[at_unit(g, s, o)]), axis=1)
        both = jnp.concatenate([both, both], axis=0)
        for q in range(cap):
            slot = q * n_cols + o
            product = jnp.dot(weight[o, q], both, preferred_element_type=jnp.float32)
            product = product[:, :LANES] + product[:, LANES:]
            product = product.reshape(CORES, tile // ROWS, ROWS, LANES)
            for c in range(CORES):
                target = meta[c, slot]
                for j in range(n_local):
                    add = jnp.where((target == float(j))[None], product[c], 0.0)
                    totals[g, s, c, j] += add.reshape(tile, LANES)

    def place(turn):
        return nearest(turn % size_z, at_z, size_z), nearest(turn // size_z, at_x, size_x)

    def consume(g, s, turn):
        sz, sx = place(turn)
        for part in range(CORES):
            o = (sz * size_x + sx) * CORES + part
            if g == 0 and s == 0:
                build(o)
            multiply(g, s, o)

    def relay_ahead(g, s):
        if turned:
            for ux in range(1, size_x):
                relay(g, s, at_z, nearest(ux, at_x, size_x), CORES - 1, spread=True)

    def relay_x(g, s, turn):
        sz, sx = place(turn)
        for part in range(CORES):
            waited = by_row(part) & (turn % size_z == 0)
            pl.when(jnp.logical_not(waited))(lambda: relay(g, s, sz, sx, part))

    def relay_z(g, s, turn):
        sz, sx = place(turn)
        for part in range(CORES):
            relay(g, s, sz, sx, part)

    def x_turns(g, s):
        @pl.loop(size_z, chips - 1)
        def _(turn):
            relay_x(g, s, turn)
            consume(g, s, turn - 1)

    def fold(g, s):
        for c in range(CORES):
            for r in range(n_rows):
                sums = [totals[g, s, c, r * per + b] for b in range(per)]
                packed[g, s, c, r] = lanes_of(*[value + roll(value) for value in sums])

    def y_copy(s, c, step):
        target = (row + step) % n_rows
        return pltpu.make_async_remote_copy(
            packed.at[0, s, c, target], partner.at[s, c, row], y_send.at[s, c, step - 1], y_recv.at[s, c, step - 1],
            device_id=(target, col), device_id_type=MESH)

    def y_sum(s, c):
        total = packed[0, s, c, row]
        for step in range(1, n_rows):
            origin = (row + n_rows - step) % n_rows
            pltpu.make_async_remote_copy(
                packed.at[0, s, c, row], partner.at[s, c, origin], y_send.at[s, c, step - 1], y_recv.at[s, c, step - 1],
                device_id=(row, col), device_id_type=MESH).wait_recv()
            total = total + partner[s, c, origin]
        return total

    def fin_copies(s):
        copies = []
        for away in range(CORES):
            c = (core + away) % CORES
            for step in range(n_rows):
                if away or step:
                    target = (row + step) % n_rows
                    i = away * n_rows + step
                    copies.append(pltpu.make_async_remote_copy(
                        packed.at[1, s, c, target], final.at[s, away, row], fin_send.at[s, i], fin_recv.at[s, i],
                        device_id=(target, chip * CORES + c), device_id_type=MESH))
        return copies

    def fin_sum(s, away):
        total = None if away else packed[1, s, core, row]
        for step in range(n_rows):
            if away or step:
                origin = (row + n_rows - step) % n_rows
                i = away * n_rows + step
                pltpu.make_async_remote_copy(
                    packed.at[1, s, core, row], final.at[s, away, origin], fin_send.at[s, i], fin_recv.at[s, i],
                    device_id=(row, col), device_id_type=MESH).wait_recv()
                piece = final[s, away, origin]
                total = piece if total is None else total + piece
        return total

    def close(g, s):
        fold(g, s)
        copies = fin_copies(s) if g else [y_copy(s, c, step) for c in range(CORES) for step in range(1, n_rows)]
        for copy in copies:
            copy.start()
        return copies

    def stats_begin(i, rows):
        filler = jnp.zeros((ROWS - len(rows), LANES), jnp.float32)
        stat_col[i, chip] = jnp.concatenate(list(rows) + [filler], axis=0)

        @pl.loop(1, chips)
        def _(step):
            pltpu.make_async_remote_copy(
                stat_col.at[i, chip], stat_col.at[i, chip], col_send.at[i], col_recv.at[i],
                device_id=(row, (chip + step) % chips * CORES + core), device_id_type=MESH).start()

    def stats_turn(i):
        many = stat_col.at[i, pl.ds(0, chips - 1)]
        pltpu.make_async_copy(many, many, col_recv.at[i]).wait()
        stat_row[i, row] = jnp.sum(stat_col[i], axis=0)

        @pl.loop(1, n_rows)
        def _(step):
            pltpu.make_async_remote_copy(
                stat_row.at[i, row], stat_row.at[i, row], row_send.at[i], row_recv.at[i],
                device_id=((row + step) % n_rows, col), device_id_type=MESH).start()

    def stats_end(i):
        many = stat_row.at[i, pl.ds(0, n_rows - 1)]
        pltpu.make_async_copy(many, many, row_recv.at[i]).wait()
        value = jnp.sum(stat_row[i], axis=0)
        return value + roll(value)

    def stats_drain(i):
        many = stat_col.at[i, pl.ds(0, chips - 1)]
        pltpu.make_async_copy(many, many, col_send.at[i]).wait()
        many = stat_row.at[i, pl.ds(0, n_rows - 1)]
        pltpu.make_async_copy(many, many, row_send.at[i]).wait()

    def over_rows(value):
        return jnp.sum(value, axis=0, keepdims=True)

    def own_units(s):
        branches(0, s, at_z, at_x, core)
        branches(0, s, at_z, at_x, core, source=other_units.at[s])

    def unit_to_mate(s):
        return pltpu.make_async_remote_copy(
            other_units.at[s], held.at[at_unit(0, s, col)], mate_send.at[s], unit_recv.at[at_unit(0, s, col)],
            device_id=(row, mate), device_id_type=MESH)

    def unit_from_mate(s):
        unit = held.at[at_unit(0, s, mate)]
        pltpu.make_async_remote_copy(
            unit, unit, mate_send.at[s], unit_recv.at[at_unit(0, s, mate)],
            device_id=(row, mate), device_id_type=MESH).wait_recv()

    for copy in own:
        copy.wait()
    mine_packed = pack(*[raw[b] for b in range(per)])
    other_packed = pack(*[own_other[b] for b in range(per)])
    for s in range(PARTS):
        held[at_unit(0, s, col)] = mine_packed[s]
        other_units[s] = other_packed[s]
        if s == 0:
            own_units(0)
    for s in range(PARTS):
        unit_to_mate(s).start()
    for copy in small:
        copy.wait()
    @pl.loop(0, slots)
    def _(slot):
        piece = bcol[slot] // per
        target = piece // n_cols * per + bcol[slot] % per
        target = jnp.where(slot < counts[0], target, -1)
        reads_low = jnp.where(low_lane, 0, 1) == brow[slot] % per
        meta[core, slot] = jnp.where(reads_low, target, -1).astype(jnp.float32)

    filler = jnp.zeros((ROWS - per, LANES), jnp.float32)
    meta[core, slots] = jnp.concatenate([diag_ref[...], filler], axis=0)
    totals[...] = jnp.zeros_like(totals)
    for copy in swaps:
        copy.start()
    for s in range(PARTS):
        unit_from_mate(s)
    squares = []
    for s in range(PARTS):
        units = [held[at_unit(0, s, chip * CORES + c)] for c in range(CORES)]
        squares.append(sum(over_rows(unit * unit) for unit in units))
    stats_begin(0, squares)
    swaps[0].wait_recv()
    for c in range(CORES):
        columns = [jnp.broadcast_to(meta[c, slots, pl.ds(b, 1)], (tile, LANES)).T for b in range(per)]
        diag[c] = lanes_of(*columns)

    def open_first():
        own_units(1)
        own_blocks.wait()
        swaps[1].wait_recv()

    middle = (at_z > 0) & (at_z + 1 < size_z)

    def gather(g, open_second, hooks):
        sent, halfway = [], []
        waiting = [[0] for _ in range(PARTS)]
        turned_stats = False
        for what, s, turn in order(g, size_z):
            if what[0] == "z" and s and not turned_stats:
                stats_turn(g)
                turned_stats = True
            if what == "own":
                open_second()
            elif what == "beside":
                relay_ahead(g, s)
            elif what == "image":
                hooks[2]()
            elif what == "close":
                for ready in waiting[s]:
                    consume(g, s, ready)
                sent += close(g, s)
                waiting[s] = []
                hooks[s]()
            else:
                came = [turn]
                if what == "z":
                    relay_z(g, s, turn)
                elif what == "x":
                    came = [turn + ux * size_z for ux in range(1, size_x)]
                    for other in came:
                        relay_x(g, s, other)
                else:
                    wanted = middle if what == "zm" else jnp.logical_not(middle)
                    pl.when(wanted)(lambda: relay_z(g, s, turn))
                    if (s, turn) not in halfway:
                        halfway.append((s, turn))
                        came = []
                for h in range(PARTS):
                    for ready in waiting[h]:
                        consume(g, h, ready)
                    waiting[h] = []
                waiting[s] += came
        return sent

    known = {}

    def nothing():
        pass

    def end_first_stats():
        stats = stats_end(0)
        known["squares"] = [stats[s:s + 1] for s in range(PARTS)]
        known["magnitude"] = [jnp.sqrt(stats[s:s + 1] / total_rows + 1e-06) for s in range(PARTS)]
        known["rows"] = []

    def make_image(s):
        image_squares, crossed = 0.0, 0.0
        magnitude = known["magnitude"][s]
        for c in range(CORES):
            unit = held[at_unit(0, s, chip * CORES + c)]
            image = (diag[c] * unit + y_sum(s, c)) / magnitude
            held[at_unit(1, s, chip * CORES + c)] = image
            branches(1, s, at_z, at_x, c)
            image_squares += over_rows(image * image)
            crossed += over_rows(image * (unit / magnitude))
        known["rows"] += [image_squares, crossed]
        to_mate(s).start()

    def to_mate(s):
        return pltpu.make_async_remote_copy(
            held.at[at_unit(1, s, mate)], cross.at[s], cross_send.at[s], cross_recv.at[s],
            device_id=(row, mate), device_id_type=MESH)

    y_sent = gather(0, open_first, (end_first_stats, nothing, lambda: make_image(0)))

    to_side = pltpu.make_async_remote_copy(
        side.at[core], side.at[core], side_sem.at[0], side_sem.at[1], device_id=(row, mate), device_id_type=MESH)

    def open_image():
        make_image(1)
        stats_begin(1, known["rows"])

    def end_second_stats():
        stats = stats_end(1)
        rows = []
        for s in range(PARTS):
            image_squares, crossed = stats[2 * s:2 * s + 1], stats[2 * s + 1:2 * s + 2]
            magnitude = known["magnitude"][s]
            basis_squares = known["squares"][s] / (magnitude * magnitude)
            projection = crossed / total_rows
            power = (image_squares - 2.0 * projection * crossed + projection * projection * basis_squares) / total_rows
            rows.append((projection, jnp.sqrt(jnp.maximum(power, 0.0) + 1e-06), magnitude))
        rows = [lanes_of(first, second) for first, second in zip(*rows)]
        side[core] = jnp.concatenate(rows + [jnp.zeros((ROWS - len(rows), LANES), jnp.float32)], axis=0)
        to_side.start()

    places = ((0, mine_at), (1, other_at))

    def image_of(s, away):
        return cross[s] if away else held[at_unit(1, s, col)]

    def make_next():
        to_side.wait_recv()
        for s in range(PARTS):
            to_mate(s).wait_recv()
        for away, at in places:
            values = side[(core + away) % CORES]
            projection, norm_new, magnitude = values[:1], values[1:2], values[2:3]
            images = pack(*[image_of(s, away) for s in range(PARTS)])
            for b in range(per):
                vector = own_other[b] if away else raw[b]
                basis = vector / magnitude
                next_ref[pl.ds(b * tile, tile), at] = (images[b] - projection * basis) / norm_new
            column_ref[:, at] = values[:2]

    def finish(s):
        for away, _ in places:
            values = side[(core + away) % CORES]
            values = lanes_of(values, roll(values)) if s == 0 else lanes_of(roll(values), values)
            image = image_of(s, away)
            result[s, away] = (diag[core] * image + fin_sum(s, away) - values[:1] * image) / values[1:2]

    sent = gather(1, open_image, (end_second_stats, make_next, nothing))

    finish(0)
    drain_units()
    for g in range(2):
        stats_drain(g)
    for copy in swaps + y_sent + [move(s) for move in (unit_to_mate, to_mate) for s in range(PARTS)] + [to_side]:
        copy.wait_send()
    finish(1)
    for away, at in places:
        values = pack(*[result[s, away] for s in range(PARTS)])
        for b in range(per):
            second_ref[pl.ds(b * tile, tile), at] = values[b]
    for copy in sent:
        copy.wait_send()


def hand_over(first, second, third, to_first, to_second, to_third, sem):
    copies = [
        pltpu.make_async_copy(source, target, sem.at[i])
        for i, (source, target) in enumerate(((first, to_first), (second, to_second), (third, to_third)))]
    for copy in copies:
        copy.start()
    for copy in copies:
        copy.wait()


def per_device(blocks, block_row, block_col, counts, diagonal, vector):
    n_rows, n_cols = lax.axis_size("row"), lax.axis_size("col")
    slots, tile, _ = blocks.shape
    mine, rhs = vector.shape
    per = mine // tile
    if rhs != CORES * LANES or tile != LANES or per != PARTS:
        raise ValueError("shapes")
    cap, chips = slots // n_cols, n_cols // CORES
    vmem = pl.BlockSpec(memory_space=pltpu.VMEM)
    anywhere = pl.BlockSpec(memory_space=pl.ANY)
    f32, dma = jnp.float32, pltpu.SemaphoreType.DMA
    unit = (tile, LANES)
    results = pl.pallas_call(
        functools.partial(kernel, n_rows, n_cols, mine * n_rows * n_cols),
        out_shape=(
            pltpu.VMEM((mine, rhs), f32),
            pltpu.VMEM((mine, rhs), f32),
            pltpu.VMEM((2, rhs), f32),
        ),
        in_specs=[anywhere] * 6,
        out_specs=(vmem, vmem, vmem),
        scratch_shapes=[
            pltpu.SMEM((slots,), jnp.int32),
            pltpu.SMEM((slots,), jnp.int32),
            pltpu.SMEM((1,), jnp.int32),
            pltpu.VMEM((per, tile), f32),
            pltpu.VMEM((CORES, slots, tile, tile), f32),
            pltpu.VMEM((2 * PARTS * n_cols,) + unit, f32),
            pltpu.VMEM((n_cols, cap, CORES * tile, 2 * tile), jnp.bfloat16),
            pltpu.VMEM((2, PARTS, CORES, n_rows * per) + unit, f32),
            pltpu.VMEM((2, PARTS, CORES, n_rows) + unit, f32),
            pltpu.VMEM((PARTS, CORES, n_rows) + unit, f32),
            pltpu.VMEM((PARTS, CORES, n_rows) + unit, f32),
            pltpu.VMEM((CORES,) + unit, f32),
            pltpu.VMEM((CORES, slots + 1, ROWS, LANES), f32),
            pltpu.VMEM((per,) + unit, f32),
            pltpu.VMEM((PARTS,) + unit, f32),
            pltpu.VMEM((per,) + unit, f32),
            pltpu.VMEM((PARTS,) + unit, f32),
            pltpu.VMEM((PARTS, CORES) + unit, f32),
            pltpu.VMEM((CORES, ROWS, LANES), f32),
            pltpu.VMEM((2, chips, ROWS, LANES), f32),
            pltpu.VMEM((2, n_rows, ROWS, LANES), f32),
            dma((2 * per + 1,)), dma((4,)), dma((PARTS,)),
            dma((2,)), dma((2,)),
            dma((4,)), dma((2 * PARTS * n_cols,)),
            dma((PARTS, CORES, n_rows - 1)), dma((PARTS, CORES, n_rows - 1)),
            dma((PARTS, CORES * n_rows)), dma((PARTS, CORES * n_rows)),
            dma((PARTS,)), dma((PARTS,)), dma((2,)),
            dma((2,)), dma((2,)), dma((2,)), dma((2,)),
        ],
        compiler_params=pltpu.CompilerParams(
            collective_id=0, has_side_effects=True, vmem_limit_bytes=60 * 1024 * 1024),
    )(block_row, block_col, counts, blocks, diagonal.reshape(per, tile), vector)
    return pl.pallas_call(
        hand_over,
        out_shape=[jax.ShapeDtypeStruct(value.shape, f32) for value in results],
        in_specs=[vmem] * 3,
        out_specs=[anywhere] * 3,
        scratch_shapes=[dma((3,))],
    )(*[pltpu.with_memory_space_constraint(value, pltpu.VMEM) for value in results])


def solution(mesh):
    spec = P(("row", "col"))
    return jax.shard_map(
        per_device,
        mesh=mesh,
        in_specs=(P(("row", "col"), None, None), spec, spec, spec, spec, P(("row", "col"), None)),
        out_specs=(P(("row", "col"), None), P(("row", "col"), None), P()),
        check_vma=False,
    )
```

```python
import functools

import jax
import jax.numpy as jnp
from jax import lax
from jax.experimental import pallas as pl
from jax.experimental.pallas import tpu as pltpu
from jax.sharding import PartitionSpec as P

MESH = pl.DeviceIdType.MESH
LANES = 128
ROWS = 8
CORES = 2
HALF = LANES // 2
PARTS = LANES // HALF


def chip_grid(chips):
    x = max(d for d in range(1, chips + 1) if chips % d == 0 and d * d <= chips)
    return chips // x, x


def nearest(turn, here, size):
    both = jnp.minimum(here, size - 1 - here)
    reach = (turn + 1) // 2
    near = jnp.where(turn % 2 == 1, here + reach, here - reach)
    far = jnp.where(here < size - 1 - here, turn, size - 1 - turn)
    return jnp.where(turn <= 2 * both, near, far)


def split(value):
    high = value.astype(jnp.bfloat16)
    low = (value - high.astype(jnp.float32)).astype(jnp.bfloat16)
    return high, low


def roll(value):
    return pltpu.roll(value, HALF, 1)


FIRST, SECOND = (
    (
        ("own", 0, 0), ("beside", 0, 0), ("z", 0, 1), ("z", 0, 2), ("z", 0, 3), ("z", 1, 1),
        ("x", 0, 0), ("x", 0, 1), ("z", 1, 2), ("beside", 1, 0), ("x", 0, 2), ("x", 0, 3),
        ("close", 0, 0), ("z", 1, 3), ("x", 1, 0), ("image", 0, 0), ("x", 1, 1), ("x", 1, 2),
        ("x", 1, 3), ("close", 1, 0),
    ),
    (
        ("own", 0, 0), ("beside", 0, 0), ("z", 0, 1), ("z", 0, 2), ("z", 0, 3), ("z", 1, 1),
        ("x", 0, 0), ("x", 0, 1), ("z", 1, 2), ("beside", 1, 0), ("x", 0, 2), ("x", 0, 3),
        ("close", 0, 0), ("z", 1, 3), ("x", 1, 0), ("x", 1, 1), ("x", 1, 2), ("x", 1, 3),
        ("close", 1, 0),
    ),
)


def order(g, size_z):
    if size_z == 4:
        return (FIRST, SECOND)[g]
    steps = [("own", 0, 0)]
    for s in range(PARTS):
        steps += [("beside", s, 0)] + [("z", s, t) for t in range(1, size_z)]
        steps += [("x", s, t) for t in range(size_z)] + [("close", s, 0)]
    return steps if g else steps[:-1] + [("image", 0, 0), steps[-1]]


def kernel(
    n_rows, n_cols, total_rows,
    brow_hbm, bcol_hbm, counts_hbm, blocks_hbm, diag_hbm, vec_hbm,
    next_ref, second_ref, column_ref,
    brow, bcol, counts, diag_ref, blocks, held, weight, totals, packed, partner, final, diag, meta, raw, other_units, own_other, cross, result, side,
    stat_col, stat_row,
    local_sem, small_sem, mate_send, swap_send, swap_recv, unit_send, unit_recv, y_send, y_recv, fin_send, fin_recv,
    cross_send, cross_recv, side_sem, col_send, col_recv, row_send, row_recv,
):
    slots, tile = blocks.shape[1], blocks.shape[2]
    cap = slots // n_cols
    per = raw.shape[0]
    n_local = n_rows * per
    chips = n_cols // CORES
    size_z, size_x = chip_grid(chips)
    row, col = lax.axis_index("row"), lax.axis_index("col")
    core, chip = col % CORES, col // CORES
    mate = chip * CORES + 1 - core
    at_x, at_z = chip % size_x, chip // size_x
    mine_at = pl.ds(pl.multiple_of(core * LANES, LANES), LANES)
    other_at = pl.ds(pl.multiple_of((1 - core) * LANES, LANES), LANES)
    low_lane = lax.broadcasted_iota(jnp.int32, (ROWS, LANES), 1) < HALF
    low_row = low_lane[:1]

    own = []
    for b in range(per):
        at = pl.ds(b * tile, tile)
        own.append(pltpu.make_async_copy(vec_hbm.at[at, mine_at], raw.at[b], local_sem.at[b]))
        own.append(pltpu.make_async_copy(vec_hbm.at[at, other_at], own_other.at[b], local_sem.at[per + b]))
    own_blocks = pltpu.make_async_copy(blocks_hbm, blocks.at[core], local_sem.at[2 * per])
    small = [
        pltpu.make_async_copy(source, target, small_sem.at[i]) for i, (source, target) in enumerate(
            ((brow_hbm, brow), (bcol_hbm, bcol), (counts_hbm, counts), (diag_hbm, diag_ref)))]
    for copy in own + small + [own_blocks]:
        copy.start()

    barrier = pltpu.get_barrier_semaphore()

    @pl.loop(1, n_cols)
    def _(step):
        pl.semaphore_signal(barrier, inc=1, device_id=(row, (col + step) % n_cols), device_id_type=MESH)

    @pl.loop(1, n_rows)
    def _(step):
        there = (row + step) % n_rows
        pl.semaphore_signal(barrier, inc=1, device_id=(there, col), device_id_type=MESH)
        pl.semaphore_signal(barrier, inc=1, device_id=(there, mate), device_id_type=MESH)

    pl.semaphore_wait(barrier, n_cols - 1 + 2 * (n_rows - 1))

    swaps = []

    def swap(source, target):
        i = len(swaps)
        swaps.append(pltpu.make_async_remote_copy(
            source, target, swap_send.at[i], swap_recv.at[i], device_id=(row, mate), device_id_type=MESH))

    swap(meta.at[core], meta.at[core])
    swap(blocks_hbm, blocks.at[core])

    def lanes_of(low, high):
        keep = low_row if low.shape[0] == 1 else low_lane
        shape = low.shape
        low, high = low.reshape((-1,) + keep.shape), high.reshape((-1,) + keep.shape)
        return jnp.where(keep[None], low, high).reshape(shape)

    def pack(first, second):
        return lanes_of(first, roll(second)), lanes_of(roll(first), second)

    def at_unit(g, s, o):
        return (g * PARTS + s) * n_cols + o

    turned = size_x > 1 and size_z % 2 == 0

    def beside(z):
        return z + 1 - 2 * (z % 2)

    def by_row(part):
        return (part == CORES - 1) if turned else (part < 0)

    def branches(g, s, sz, sx, part, spread=False, source=None):
        o = (sz * size_x + sx) * CORES + part
        there = core if source is None else 1 - core
        along_z = at_x == sx
        along_x = jnp.logical_not(by_row(part) & (sz == beside(at_z)))
        targets = [
            (0, along_z & (at_z >= sz) & (at_z + 1 < size_z), at_x, at_z + 1),
            (1, along_z & (at_z <= sz) & (at_z >= 1), at_x, at_z - 1),
            (2, along_x & (at_x >= sx) & (at_x + 1 < size_x), at_x + 1, at_z),
            (3, along_x & (at_x <= sx) & (at_x >= 1), at_x - 1, at_z),
        ]
        if spread:
            targets = targets[2:]
            targets += [(0, at_z % 2 == 0, at_x, at_z + 1), (1, at_z % 2 == 1, at_x, at_z - 1)]
        piece = held.at[at_unit(g, s, o)]
        source = piece if source is None else source
        for i, wanted, tx, tz in targets:
            def go(i=i, tx=tx, tz=tz):
                pltpu.make_async_remote_copy(
                    source, piece, unit_send.at[i], unit_recv.at[at_unit(g, s, o)],
                    device_id=(row, (tz * size_x + tx) * CORES + there), device_id_type=MESH).start()
            pl.when(wanted)(go)

    def drain_units():
        extra = size_x - 1 if turned else 0

        def wait(i, n, wanted):
            def go():
                many = held.at[pl.ds(0, 2 * PARTS * n)]
                pltpu.make_async_copy(many, many, unit_send.at[i]).wait()
            pl.when(wanted)(go)

        for v in range(size_z):
            if v + 1 < size_z:
                wait(0, (v + 1) * CORES + (extra if v % 2 == 0 else 0), at_z == v)
            if v:
                wait(1, (size_z - v) * CORES + (extra if v % 2 else 0), at_z == v)
        for v in range(size_x - 1):
            n = (v + 1) * (CORES * size_z - (1 if turned else 0))
            wait(2, n, at_x == v)
            wait(3, n, at_x == size_x - 1 - v)

    def relay(g, s, sz, sx, part, spread=False):
        unit = at_unit(g, s, (sz * size_x + sx) * CORES + part)
        piece = held.at[unit]
        pltpu.make_async_remote_copy(
            piece, piece, unit_send.at[0], unit_recv.at[unit],
            device_id=(row, col), device_id_type=MESH).wait_recv()
        branches(g, s, sz, sx, part, spread)

    def build(o):
        for q in range(cap):
            slot = q * n_cols + o
            for c in range(CORES):
                high, low = split(blocks[c, slot].T)
                weight[o, q, pl.ds(c * tile, tile), pl.ds(0, tile)] = high
                weight[o, q, pl.ds(c * tile, tile), pl.ds(tile, tile)] = low

    def multiply(g, s, o):
        both = jnp.concatenate(split(held[at_unit(g, s, o)]), axis=1)
        both = jnp.concatenate([both, both], axis=0)
        for q in range(cap):
            slot = q * n_cols + o
            product = jnp.dot(weight[o, q], both, preferred_element_type=jnp.float32)
            product = product[:, :LANES] + product[:, LANES:]
            product = product.reshape(CORES, tile // ROWS, ROWS, LANES)
            for c in range(CORES):
                target = meta[c, slot]
                for j in range(n_local):
                    add = jnp.where((target == float(j))[None], product[c], 0.0)
                    totals[g, s, c, j] += add.reshape(tile, LANES)

    def place(turn):
        return nearest(turn % size_z, at_z, size_z), nearest(turn // size_z, at_x, size_x)

    def consume(g, s, turn):
        sz, sx = place(turn)
        for part in range(CORES):
            o = (sz * size_x + sx) * CORES + part
            if g == 0 and s == 0:
                build(o)
            multiply(g, s, o)

    def relay_ahead(g, s):
        if turned:
            for ux in range(1, size_x):
                relay(g, s, at_z, nearest(ux, at_x, size_x), CORES - 1, spread=True)

    def relay_x(g, s, turn):
        sz, sx = place(turn)
        for part in range(CORES):
            waited = by_row(part) & (turn % size_z == 0)
            pl.when(jnp.logical_not(waited))(lambda: relay(g, s, sz, sx, part))

    def relay_z(g, s, turn):
        sz, sx = place(turn)
        for part in range(CORES):
            relay(g, s, sz, sx, part)

    def x_turns(g, s):
        @pl.loop(size_z, chips - 1)
        def _(turn):
            relay_x(g, s, turn)
            consume(g, s, turn - 1)

    def fold(g, s):
        for c in range(CORES):
            for r in range(n_rows):
                sums = [totals[g, s, c, r * per + b] for b in range(per)]
                packed[g, s, c, r] = lanes_of(*[value + roll(value) for value in sums])

    def y_copy(s, c, step):
        target = (row + step) % n_rows
        return pltpu.make_async_remote_copy(
            packed.at[0, s, c, target], partner.at[s, c, row], y_send.at[s, c, step - 1], y_recv.at[s, c, step - 1],
            device_id=(target, col), device_id_type=MESH)

    def y_sum(s, c):
        total = packed[0, s, c, row]
        for step in range(1, n_rows):
            origin = (row + n_rows - step) % n_rows
            pltpu.make_async_remote_copy(
                packed.at[0, s, c, row], partner.at[s, c, origin], y_send.at[s, c, step - 1], y_recv.at[s, c, step - 1],
                device_id=(row, col), device_id_type=MESH).wait_recv()
            total = total + partner[s, c, origin]
        return total

    def fin_copies(s):
        copies = []
        for away in range(CORES):
            c = (core + away) % CORES
            for step in range(n_rows):
                if away or step:
                    target = (row + step) % n_rows
                    i = away * n_rows + step
                    copies.append(pltpu.make_async_remote_copy(
                        packed.at[1, s, c, target], final.at[s, away, row], fin_send.at[s, i], fin_recv.at[s, i],
                        device_id=(target, chip * CORES + c), device_id_type=MESH))
        return copies

    def fin_sum(s, away):
        total = None if away else packed[1, s, core, row]
        for step in range(n_rows):
            if away or step:
                origin = (row + n_rows - step) % n_rows
                i = away * n_rows + step
                pltpu.make_async_remote_copy(
                    packed.at[1, s, core, row], final.at[s, away, origin], fin_send.at[s, i], fin_recv.at[s, i],
                    device_id=(row, col), device_id_type=MESH).wait_recv()
                piece = final[s, away, origin]
                total = piece if total is None else total + piece
        return total

    def close(g, s):
        fold(g, s)
        copies = fin_copies(s) if g else [y_copy(s, c, step) for c in range(CORES) for step in range(1, n_rows)]
        for copy in copies:
            copy.start()
        return copies

    def stats_begin(i, rows):
        filler = jnp.zeros((ROWS - len(rows), LANES), jnp.float32)
        stat_col[i, chip] = jnp.concatenate(list(rows) + [filler], axis=0)

        @pl.loop(1, chips)
        def _(step):
            pltpu.make_async_remote_copy(
                stat_col.at[i, chip], stat_col.at[i, chip], col_send.at[i], col_recv.at[i],
                device_id=(row, (chip + step) % chips * CORES + core), device_id_type=MESH).start()

    def stats_turn(i):
        many = stat_col.at[i, pl.ds(0, chips - 1)]
        pltpu.make_async_copy(many, many, col_recv.at[i]).wait()
        stat_row[i, row] = jnp.sum(stat_col[i], axis=0)

        @pl.loop(1, n_rows)
        def _(step):
            pltpu.make_async_remote_copy(
                stat_row.at[i, row], stat_row.at[i, row], row_send.at[i], row_recv.at[i],
                device_id=((row + step) % n_rows, col), device_id_type=MESH).start()

    def stats_end(i):
        many = stat_row.at[i, pl.ds(0, n_rows - 1)]
        pltpu.make_async_copy(many, many, row_recv.at[i]).wait()
        value = jnp.sum(stat_row[i], axis=0)
        return value + roll(value)

    def stats_drain(i):
        many = stat_col.at[i, pl.ds(0, chips - 1)]
        pltpu.make_async_copy(many, many, col_send.at[i]).wait()
        many = stat_row.at[i, pl.ds(0, n_rows - 1)]
        pltpu.make_async_copy(many, many, row_send.at[i]).wait()

    def over_rows(value):
        return jnp.sum(value, axis=0, keepdims=True)

    def own_units(s):
        branches(0, s, at_z, at_x, core)
        branches(0, s, at_z, at_x, core, source=other_units.at[s])

    def unit_to_mate(s):
        return pltpu.make_async_remote_copy(
            other_units.at[s], held.at[at_unit(0, s, col)], mate_send.at[s], unit_recv.at[at_unit(0, s, col)],
            device_id=(row, mate), device_id_type=MESH)

    def unit_from_mate(s):
        unit = held.at[at_unit(0, s, mate)]
        pltpu.make_async_remote_copy(
            unit, unit, mate_send.at[s], unit_recv.at[at_unit(0, s, mate)],
            device_id=(row, mate), device_id_type=MESH).wait_recv()

    for copy in own:
        copy.wait()
    mine_packed = pack(*[raw[b] for b in range(per)])
    other_packed = pack(*[own_other[b] for b in range(per)])
    for s in range(PARTS):
        held[at_unit(0, s, col)] = mine_packed[s]
        other_units[s] = other_packed[s]
        if s == 0:
            own_units(0)
    for s in range(PARTS):
        unit_to_mate(s).start()
    for copy in small:
        copy.wait()
    @pl.loop(0, slots)
    def _(slot):
        piece = bcol[slot] // per
        target = piece // n_cols * per + bcol[slot] % per
        target = jnp.where(slot < counts[0], target, -1)
        reads_low = jnp.where(low_lane, 0, 1) == brow[slot] % per
        meta[core, slot] = jnp.where(reads_low, target, -1).astype(jnp.float32)

    filler = jnp.zeros((ROWS - per, LANES), jnp.float32)
    meta[core, slots] = jnp.concatenate([diag_ref[...], filler], axis=0)
    totals[...] = jnp.zeros_like(totals)
    for copy in swaps:
        copy.start()
    for s in range(PARTS):
        unit_from_mate(s)
    squares = []
    for s in range(PARTS):
        units = [held[at_unit(0, s, chip * CORES + c)] for c in range(CORES)]
        squares.append(sum(over_rows(unit * unit) for unit in units))
    stats_begin(0, squares)
    swaps[0].wait_recv()
    for c in range(CORES):
        columns = [jnp.broadcast_to(meta[c, slots, pl.ds(b, 1)], (tile, LANES)).T for b in range(per)]
        diag[c] = lanes_of(*columns)

    def open_first():
        own_units(1)
        own_blocks.wait()
        swaps[1].wait_recv()

    middle = (at_z > 0) & (at_z + 1 < size_z)

    def gather(g, open_second, hooks):
        sent, halfway = [], []
        waiting = [[0] for _ in range(PARTS)]
        turned_stats = False
        for what, s, turn in order(g, size_z):
            if what[0] == "z" and s and not turned_stats:
                stats_turn(g)
                turned_stats = True
            if what == "own":
                open_second()
            elif what == "beside":
                relay_ahead(g, s)
            elif what == "image":
                hooks[2]()
            elif what == "close":
                for ready in waiting[s]:
                    consume(g, s, ready)
                sent += close(g, s)
                waiting[s] = []
                hooks[s]()
            else:
                came = [turn]
                if what == "z":
                    relay_z(g, s, turn)
                elif what == "x":
                    came = [turn + ux * size_z for ux in range(1, size_x)]
                    for other in came:
                        relay_x(g, s, other)
                else:
                    wanted = middle if what == "zm" else jnp.logical_not(middle)
                    pl.when(wanted)(lambda: relay_z(g, s, turn))
                    if (s, turn) not in halfway:
                        halfway.append((s, turn))
                        came = []
                for h in range(PARTS):
                    for ready in waiting[h]:
                        consume(g, h, ready)
                    waiting[h] = []
                waiting[s] += came
        return sent

    known = {}

    def nothing():
        pass

    def end_first_stats():
        stats = stats_end(0)
        known["squares"] = [stats[s:s + 1] for s in range(PARTS)]
        known["magnitude"] = [jnp.sqrt(stats[s:s + 1] / total_rows + 1e-06) for s in range(PARTS)]
        known["rows"] = []

    def make_image(s):
        image_squares, crossed = 0.0, 0.0
        magnitude = known["magnitude"][s]
        for c in range(CORES):
            unit = held[at_unit(0, s, chip * CORES + c)]
            image = (diag[c] * unit + y_sum(s, c)) / magnitude
            held[at_unit(1, s, chip * CORES + c)] = image
            branches(1, s, at_z, at_x, c)
            image_squares += over_rows(image * image)
            crossed += over_rows(image * (unit / magnitude))
        known["rows"] += [image_squares, crossed]
        to_mate(s).start()

    def to_mate(s):
        return pltpu.make_async_remote_copy(
            held.at[at_unit(1, s, mate)], cross.at[s], cross_send.at[s], cross_recv.at[s],
            device_id=(row, mate), device_id_type=MESH)

    y_sent = gather(0, open_first, (end_first_stats, nothing, lambda: make_image(0)))

    to_side = pltpu.make_async_remote_copy(
        side.at[core], side.at[core], side_sem.at[0], side_sem.at[1], device_id=(row, mate), device_id_type=MESH)

    def open_image():
        make_image(1)
        stats_begin(1, known["rows"])

    def end_second_stats():
        stats = stats_end(1)
        rows = []
        for s in range(PARTS):
            image_squares, crossed = stats[2 * s:2 * s + 1], stats[2 * s + 1:2 * s + 2]
            magnitude = known["magnitude"][s]
            basis_squares = known["squares"][s] / (magnitude * magnitude)
            projection = crossed / total_rows
            power = (image_squares - 2.0 * projection * crossed + projection * projection * basis_squares) / total_rows
            rows.append((projection, jnp.sqrt(jnp.maximum(power, 0.0) + 1e-06), magnitude))
        rows = [lanes_of(first, second) for first, second in zip(*rows)]
        side[core] = jnp.concatenate(rows + [jnp.zeros((ROWS - len(rows), LANES), jnp.float32)], axis=0)
        to_side.start()

    places = ((0, mine_at), (1, other_at))

    def image_of(s, away):
        return cross[s] if away else held[at_unit(1, s, col)]

    def make_next():
        to_side.wait_recv()
        for s in range(PARTS):
            to_mate(s).wait_recv()
        for away, at in places:
            values = side[(core + away) % CORES]
            projection, norm_new, magnitude = values[:1], values[1:2], values[2:3]
            images = pack(*[image_of(s, away) for s in range(PARTS)])
            for b in range(per):
                vector = own_other[b] if away else raw[b]
                basis = vector / magnitude
                next_ref[pl.ds(b * tile, tile), at] = (images[b] - projection * basis) / norm_new
            column_ref[:, at] = values[:2]

    def finish(s):
        for away, _ in places:
            values = side[(core + away) % CORES]
            values = lanes_of(values, roll(values)) if s == 0 else lanes_of(roll(values), values)
            image = image_of(s, away)
            result[s, away] = (diag[core] * image + fin_sum(s, away) - values[:1] * image) / values[1:2]

    sent = gather(1, open_image, (end_second_stats, make_next, nothing))

    finish(0)
    drain_units()
    for g in range(2):
        stats_drain(g)
    for copy in swaps + y_sent + [move(s) for move in (unit_to_mate, to_mate) for s in range(PARTS)] + [to_side]:
        copy.wait_send()
    finish(1)
    for away, at in places:
        values = pack(*[result[s, away] for s in range(PARTS)])
        for b in range(per):
            second_ref[pl.ds(b * tile, tile), at] = values[b]
    for copy in sent:
        copy.wait_send()


def hand_over(first, second, third, to_first, to_second, to_third, sem):
    copies = [
        pltpu.make_async_copy(source, target, sem.at[i])
        for i, (source, target) in enumerate(((first, to_first), (second, to_second), (third, to_third)))]
    for copy in copies:
        copy.start()
    for copy in copies:
        copy.wait()


def per_device(blocks, block_row, block_col, counts, diagonal, vector):
    n_rows, n_cols = lax.axis_size("row"), lax.axis_size("col")
    slots, tile, _ = blocks.shape
    mine, rhs = vector.shape
    per = mine // tile
    if rhs != CORES * LANES or tile != LANES or per != PARTS:
        raise ValueError("shapes")
    cap, chips = slots // n_cols, n_cols // CORES
    vmem = pl.BlockSpec(memory_space=pltpu.VMEM)
    anywhere = pl.BlockSpec(memory_space=pl.ANY)
    f32, dma = jnp.float32, pltpu.SemaphoreType.DMA
    unit = (tile, LANES)
    results = pl.pallas_call(
        functools.partial(kernel, n_rows, n_cols, mine * n_rows * n_cols),
        out_shape=(
            pltpu.VMEM((mine, rhs), f32),
            pltpu.VMEM((mine, rhs), f32),
            pltpu.VMEM((2, rhs), f32),
        ),
        in_specs=[anywhere] * 6,
        out_specs=(vmem, vmem, vmem),
        scratch_shapes=[
            pltpu.SMEM((slots,), jnp.int32),
            pltpu.SMEM((slots,), jnp.int32),
            pltpu.SMEM((1,), jnp.int32),
            pltpu.VMEM((per, tile), f32),
            pltpu.VMEM((CORES, slots, tile, tile), f32),
            pltpu.VMEM((2 * PARTS * n_cols,) + unit, f32),
            pltpu.VMEM((n_cols, cap, CORES * tile, 2 * tile), jnp.bfloat16),
            pltpu.VMEM((2, PARTS, CORES, n_rows * per) + unit, f32),
            pltpu.VMEM((2, PARTS, CORES, n_rows) + unit, f32),
            pltpu.VMEM((PARTS, CORES, n_rows) + unit, f32),
            pltpu.VMEM((PARTS, CORES, n_rows) + unit, f32),
            pltpu.VMEM((CORES,) + unit, f32),
            pltpu.VMEM((CORES, slots + 1, ROWS, LANES), f32),
            pltpu.VMEM((per,) + unit, f32),
            pltpu.VMEM((PARTS,) + unit, f32),
            pltpu.VMEM((per,) + unit, f32),
            pltpu.VMEM((PARTS,) + unit, f32),
            pltpu.VMEM((PARTS, CORES) + unit, f32),
            pltpu.VMEM((CORES, ROWS, LANES), f32),
            pltpu.VMEM((2, chips, ROWS, LANES), f32),
            pltpu.VMEM((2, n_rows, ROWS, LANES), f32),
            dma((2 * per + 1,)), dma((4,)), dma((PARTS,)),
            dma((2,)), dma((2,)),
            dma((4,)), dma((2 * PARTS * n_cols,)),
            dma((PARTS, CORES, n_rows - 1)), dma((PARTS, CORES, n_rows - 1)),
            dma((PARTS, CORES * n_rows)), dma((PARTS, CORES * n_rows)),
            dma((PARTS,)), dma((PARTS,)), dma((2,)),
            dma((2,)), dma((2,)), dma((2,)), dma((2,)),
        ],
        compiler_params=pltpu.CompilerParams(
            collective_id=0, has_side_effects=True, vmem_limit_bytes=60 * 1024 * 1024),
    )(block_row, block_col, counts, blocks, diagonal.reshape(per, tile), vector)
    return pl.pallas_call(
        hand_over,
        out_shape=[jax.ShapeDtypeStruct(value.shape, f32) for value in results],
        in_specs=[vmem] * 3,
        out_specs=[anywhere] * 3,
        scratch_shapes=[dma((3,))],
    )(*[pltpu.with_memory_space_constraint(value, pltpu.VMEM) for value in results])


def solution(mesh):
    spec = P(("row", "col"))
    return jax.shard_map(
        per_device,
        mesh=mesh,
        in_specs=(P(("row", "col"), None, None), spec, spec, spec, spec, P(("row", "col"), None)),
        out_specs=(P(("row", "col"), None), P(("row", "col"), None), P()),
        check_vma=False,
    )
```
